32 devices in a mesh: sub: 16 (over z, y, x), freq: 2 (over core).
Axes of the slice: x: 2, y: 2, z: 4, core: 2. Of those that a mesh axis runs over, the one named last changes fastest.
Arguments:
- facet_image: bfloat16 [2, 1024, 1024], P('freq', 'sub'), may hold values from -0.015625 to 0.015625
- facet_tile: int32 [2, 2], P('freq'), may hold values from 0 to 63
- subgrid_cell: int32 [16, 2], P('sub'), may hold values from 0 to 65535
- row_subgrid: int32 [32768], P(('sub', 'freq')), may hold values from 0 to 15, as said below
- row_uv: float32 [2, 32768], P(None, ('sub', 'freq')), may hold values from 0 to 256
- observed: float32 [2, 32768], P(None, ('sub', 'freq')), may hold values from -6 to 6
Outputs:
- residual_vis: float32 [2, 32768], P(None, ('sub', 'freq'))
The draws below stay inside these ranges and needn't reach their ends.
Inputs may be any that keep to these rules, and one draw needn't show every extreme that they name: `row_subgrid`: the subgrid whose cells hold the row's visibility; the rows of one device's block (aligned blocks of 1024 rows) name exactly 8 cyclically consecutive subgrids c, c + 1, ..., c + 8 - 1 (mod 16).
All inputs are finite; a program needn't handle non-finite values.
Results may differ from the reference program's by a relative error of at most 0.0035.
Values may be sent and summed in bfloat16 or wider, within the bound.
A program may use at most 64 MiB of HBM per device.

```python
import math
import jax
import jax.numpy as jnp
from jax import lax

SG = 256
FACET = 1024
NIMG = 65536
SPAN = 8
ROWS_DEV = 1024
NFACET = 2
NSUBGRID = 16
ROWS = 32768


def draw_row_subgrid(key, part):
    blocks = ROWS // ROWS_DEV
    keys = jax.random.split(jax.random.fold_in(key, 11), 3)
    first = jax.random.randint(keys[0], (blocks,), 0, NSUBGRID)
    second = jax.random.randint(keys[1], (blocks,), 0, NSUBGRID)
    center = jnp.minimum(first, second)
    center = center.at[0].set(NSUBGRID - 1)
    offset = jax.random.randint(keys[2], (blocks, ROWS_DEV), 0, SPAN)
    offset = offset.at[:, 0].set(0).at[:, 1].set(SPAN - 1)
    offset = offset.at[0, 2].set(1)
    labels = ((center[:, None] + offset) % NSUBGRID).reshape(blocks * ROWS_DEV)
    return labels.astype(jnp.int32)


def plant(result, key, low, largest):
    longest = result.shape.index(max(result.shape))
    spots = []
    for shift in (0, 1):
        where = [jax.random.randint(jax.random.fold_in(key, axis), (), 0, length) for axis, length in enumerate(result.shape)]
        where[longest] = (where[longest] + shift) % result.shape[longest]
        spots.append(tuple(where))
    return result.at[spots[0]].set(low).at[spots[1]].set(largest)


def block_levels(key, dims, pieces, least, top_value):
    def one(dim, parts):
        heights = jax.random.uniform(jax.random.fold_in(jax.random.fold_in(key, 6), dim), (parts,), jnp.float32, least / len(pieces), top_value / len(pieces))
        return jnp.repeat(jnp.exp(heights), dims[dim] // parts).reshape((-1,) + (1,) * (len(dims) - dim - 1))

    level = one(*pieces[0])
    for cut in pieces[1:]:
        level = level * one(*cut)
    return level


def bell_draw(own_key, dims, width, reach, cuts=(), kind=jnp.bfloat16):
    loudness = block_levels(own_key, dims, cuts, -0.22, 0.18) if cuts else 1.0
    entries = jax.random.normal(own_key, dims, jnp.float32) * width * loudness
    return jnp.minimum(jnp.maximum(entries, -reach), reach).astype(kind)


def setup_inputs(seed: int = 0) -> dict:
    key_of = jax.random.split(jax.random.key(seed), 7)
    return {
        "facet_image": bell_draw(key_of[0], (NFACET, FACET, FACET), (1.0 / FACET), 0.015625, ((0, 2), (1, 16))),
        "facet_tile": plant(jax.random.randint(key_of[1], (NFACET, 2), 0, NIMG // FACET), jax.random.fold_in(key_of[1], 1), 0, (NIMG // FACET) - 1).astype(jnp.int32),
        "subgrid_cell": plant(jax.random.randint(key_of[2], (NSUBGRID, 2), 0, NIMG), jax.random.fold_in(key_of[2], 1), 0, NIMG - 1).astype(jnp.int32),
        "row_subgrid": draw_row_subgrid(jax.random.fold_in(key_of[6], 71), 0),
        "row_uv": jnp.clip(256.0 * jax.random.uniform(key_of[4], (2, ROWS), jnp.float32) ** block_levels(key_of[4], (2, ROWS), ((1, 32),), -0.2, 0.2), 0.0, 256.0),
        "observed": bell_draw(key_of[5], (2, ROWS), 1.0, 6.0, ((1, 32),), jnp.float32),
    }


TWO_PI = 2.0 * math.pi


def facet_window(count):
    position = (2.0 * jnp.arange(count, dtype=jnp.float32) + 1.0) / count - 1.0
    return 1.0 - 0.75 * position * position


def grid_taper(count):
    position = (2.0 * jnp.arange(count, dtype=jnp.float32) + 1.0) / count - 1.0
    return 1.0 - 0.5 * position * position


def phase_table(first_cells, second_cells, weights):
    product = (first_cells[:, None] * second_cells[None, :]) % NIMG
    angle = (TWO_PI / NIMG) * product.astype(jnp.float32)
    real_part = (weights * jnp.cos(angle)).astype(jnp.bfloat16)
    imag_part = (-weights * jnp.sin(angle)).astype(jnp.bfloat16)
    return real_part, imag_part


def full_dot(left, right):
    return jnp.dot(left.astype(jnp.float32), right.astype(jnp.float32), preferred_element_type=jnp.float32)


def full_dot_trans(left, right):
    return lax.dot_general(left.astype(jnp.float32), right.astype(jnp.float32), (((1,), (1,)), ((), ())), preferred_element_type=jnp.float32)


def idg_image(grid_real, grid_imag, product):
    spots = jnp.arange(SG, dtype=jnp.int32)
    angle = (TWO_PI / SG) * ((spots[:, None] * spots[None, :]) % SG).astype(jnp.float32)
    kernel_real = jnp.cos(angle).astype(jnp.bfloat16)
    kernel_imag = jnp.sin(angle).astype(jnp.bfloat16)
    kernel_both = jnp.concatenate([kernel_real, kernel_imag], axis=1)
    first_real = product(grid_real, kernel_both)
    first_imag = product(grid_imag, kernel_both)
    half_real = (first_real[:, :SG] - first_imag[:, SG:]).astype(jnp.bfloat16)
    half_imag = (first_real[:, SG:] + first_imag[:, :SG]).astype(jnp.bfloat16)
    half_both = jnp.concatenate([half_real, half_imag], axis=1)
    second_real = product(kernel_real, half_both)
    second_imag = product(kernel_imag, half_both)
    taper = grid_taper(SG)
    scale = taper[:, None] * taper[None, :] / (SG * SG)
    image_real = ((second_real[:, :SG] - second_imag[:, SG:]) * scale).astype(jnp.bfloat16)
    image_imag = ((second_real[:, SG:] + second_imag[:, :SG]) * scale).astype(jnp.bfloat16)
    return jnp.concatenate([image_real, image_imag], axis=0)


def degrid(image_both, match, u_pos, v_pos, product_trans):
    spots = jnp.arange(SG, dtype=jnp.float32)
    angle_u = (TWO_PI / SG) * u_pos[:, None] * spots[None, :]
    along_real = jnp.cos(angle_u).astype(jnp.bfloat16)
    along_imag = (-jnp.sin(angle_u)).astype(jnp.bfloat16)
    first = product_trans(along_real, image_both)
    second = product_trans(along_imag, image_both)
    inner_real = first[:, :SG] - second[:, SG:]
    inner_imag = first[:, SG:] + second[:, :SG]
    angle_v = (TWO_PI / SG) * v_pos[:, None] * spots[None, :]
    cross_real = jnp.cos(angle_v)
    cross_imag = -jnp.sin(angle_v)
    vis_real = jnp.sum(inner_real * cross_real - inner_imag * cross_imag, axis=1)
    vis_imag = jnp.sum(inner_real * cross_imag + inner_imag * cross_real, axis=1)
    return jnp.where(match[None, :], jnp.stack([vis_real, vis_imag]), 0.0)


def reference(facet_image, facet_tile, subgrid_cell, row_subgrid, row_uv, observed):
    window = facet_window(FACET)
    cells = jnp.arange(FACET, dtype=jnp.int32)
    spots = jnp.arange(SG, dtype=jnp.int32)

    def one_subgrid(cell):
        def one_facet(carry, item):
            image, tile = item
            col_real, col_imag = phase_table(tile[0] * FACET + cells, cell[0] + spots, window[:, None])
            spectra = full_dot(image, jnp.concatenate([col_real, col_imag], axis=1)).astype(jnp.bfloat16)
            row_real, row_imag = phase_table(cell[1] + spots, tile[1] * FACET + cells, window[None, :])
            first = full_dot(row_real, spectra)
            second = full_dot(row_imag, spectra)
            return (carry[0] + (first[:, :SG] - second[:, SG:]), carry[1] + (first[:, SG:] + second[:, :SG])), None

        empty = jnp.zeros((SG, SG), jnp.float32)
        sums, unused = lax.scan(one_facet, (empty, empty), (facet_image, facet_tile))
        return idg_image(sums[0].astype(jnp.bfloat16), sums[1].astype(jnp.bfloat16), full_dot)

    images = lax.map(one_subgrid, subgrid_cell)
    owner_count = images.shape[0]
    blocks = row_subgrid.shape[0] // ROWS_DEV
    ids_blocks = row_subgrid.reshape(blocks, ROWS_DEV)
    u_blocks = row_uv[0].reshape(blocks, ROWS_DEV)
    v_blocks = row_uv[1].reshape(blocks, ROWS_DEV)

    def one_block(item):
        ids, u_pos, v_pos = item

        def one_owner(total, owner):
            match = ids == owner
            contribution = lax.cond(jnp.any(match), lambda: degrid(images[owner], match, u_pos, v_pos, full_dot_trans), lambda: jnp.zeros((2, ROWS_DEV), jnp.float32))
            return total + contribution, None

        total, unused = lax.scan(one_owner, jnp.zeros((2, ROWS_DEV), jnp.float32), jnp.arange(owner_count, dtype=jnp.int32))
        return total

    predicted = lax.map(one_block, (ids_blocks, u_blocks, v_blocks))
    predicted = jnp.transpose(predicted, (1, 0, 2)).reshape(2, blocks * ROWS_DEV)
    return observed - predicted
```

```python
import math

import numpy as np
import jax
import jax.numpy as jnp
from jax import lax
from jax.experimental import pallas as pl
from jax.experimental.pallas import tpu as pltpu
from jax.sharding import PartitionSpec as P

SG = 256
FACET = 1024
NIMG = 65536
CHUNK = 256
HALF_PI = math.pi / 2.0


def nt_dot(left, right):
    return lax.dot_general(
        left, right, (((1,), (1,)), ((), ())), preferred_element_type=jnp.float32
    )


def plain_dot(left, right):
    return jnp.dot(left, right, preferred_element_type=jnp.float32)


def unit_root(quarters):
    whole = jnp.floor(quarters + 0.5)
    angle = HALF_PI * (quarters - whole)
    turn = whole.astype(jnp.int32)
    sq = angle * angle
    sin_part = angle * (
        1.0 + sq * (-1.0 / 6.0 + sq * (1.0 / 120.0 + sq * (-1.0 / 5040.0 + sq * (1.0 / 362880.0))))
    )
    cos_part = 1.0 + sq * (
        -0.5 + sq * (1.0 / 24.0 + sq * (-1.0 / 720.0 + sq * (1.0 / 40320.0)))
    )
    odd = (turn & 1) == 1
    cos_turned = jnp.where(odd, sin_part, cos_part)
    sin_turned = jnp.where(odd, cos_part, sin_part)
    cos_out = jnp.where(((turn + 1) & 2) == 2, -cos_turned, cos_turned)
    sin_out = jnp.where((turn & 2) == 2, -sin_turned, sin_turned)
    return cos_out, -sin_out


def outer_product(coarse, fine):
    rows, lanes = coarse[0].shape
    cr, ci = coarse[0][:, None, :], coarse[1][:, None, :]
    fr, fi = fine[0][None, :, :], fine[1][None, :, :]
    real_part = (cr * fr - ci * fi).reshape(rows * 8, lanes)
    imag_part = (cr * fi + ci * fr).reshape(rows * 8, lanes)
    return real_part, imag_part


def window_table(first_cell, first_pixel):
    lanes = lax.broadcasted_iota(jnp.int32, (8, FACET), 1)
    fine_rows = lax.broadcasted_iota(jnp.int32, (8, FACET), 0)
    coarse_lanes = lax.broadcasted_iota(jnp.int32, (SG // 8, FACET), 1)
    coarse_rows = lax.broadcasted_iota(jnp.int32, (SG // 8, FACET), 0)
    position = (2.0 * lanes.astype(jnp.float32) + 1.0) / FACET - 1.0
    weights = 1.0 - 0.75 * position * position
    fine_phase = (fine_rows * (first_pixel + lanes)) & (NIMG - 1)
    coarse_phase = ((first_cell + 8 * coarse_rows) * (first_pixel + coarse_lanes)) & (NIMG - 1)
    fine = unit_root(fine_phase.astype(jnp.float32) * (4.0 / NIMG))
    coarse = unit_root(coarse_phase.astype(jnp.float32) * (4.0 / NIMG))
    real_part, imag_part = outer_product(coarse, (weights * fine[0], weights * fine[1]))
    return real_part.astype(jnp.bfloat16), imag_part.astype(jnp.bfloat16)


def facet_kernel(tile_ref, cell_ref, image_ref, out_ref, col_ref, spectra_ref):
    col_real, col_imag = window_table(cell_ref[0, 0], tile_ref[0, 0] * FACET)
    col_ref[:SG] = col_real
    col_ref[SG:] = col_imag
    for part in range(4):
        rows = slice(part * 256, part * 256 + 256)
        spectra_ref[:, rows] = nt_dot(col_ref[...], image_ref[rows]).astype(jnp.bfloat16)
    row_real, row_imag = window_table(cell_ref[0, 1], tile_ref[0, 1] * FACET)
    first = nt_dot(row_real, spectra_ref[...])
    second = nt_dot(row_imag, spectra_ref[...])
    out_ref[:, :SG] = first[:, :SG] - second[:, SG:]
    out_ref[:, SG:] = first[:, SG:] + second[:, :SG]


def subgrid_image(grid_real, grid_imag, kernel_real, kernel_imag):
    kernel_both = jnp.concatenate([kernel_real, kernel_imag], axis=1)
    first_real = plain_dot(grid_real, kernel_both)
    first_imag = plain_dot(grid_imag, kernel_both)
    half_real = (first_real[:, :SG] - first_imag[:, SG:]).astype(jnp.bfloat16)
    half_imag = (first_real[:, SG:] + first_imag[:, :SG]).astype(jnp.bfloat16)
    half_both = jnp.concatenate([half_real, half_imag], axis=1)
    second_real = plain_dot(kernel_real, half_both)
    second_imag = plain_dot(kernel_imag, half_both)

    def taper(axis):
        cells = lax.broadcasted_iota(jnp.int32, (SG, SG), axis).astype(jnp.float32)
        position = (2.0 * cells + 1.0) / SG - 1.0
        return 1.0 - 0.5 * position * position

    scale = taper(0) * taper(1) / (SG * SG)
    image_real = ((second_real[:, :SG] - second_imag[:, SG:]) * scale).astype(jnp.bfloat16)
    image_imag = ((second_real[:, SG:] + second_imag[:, :SG]) * scale).astype(jnp.bfloat16)
    return image_real, image_imag


def powers(position, lanes):
    quarters = position * (4.0 / SG)
    steps = lax.broadcasted_iota(jnp.int32, (8, lanes), 0).astype(jnp.float32)
    fine = unit_root(quarters * steps)
    mid = unit_root(quarters * (8.0 * steps))
    wide = unit_root(quarters * (64.0 * steps))
    real_parts, imag_parts = [], []
    for q in range(SG // 64):
        wr, wi = wide[0][q : q + 1], wide[1][q : q + 1]
        real_parts.append(mid[0] * wr - mid[1] * wi)
        imag_parts.append(mid[0] * wi + mid[1] * wr)
    return (jnp.concatenate(real_parts), jnp.concatenate(imag_parts)), fine


def degrid_kernel(grid_ref, dft_ref, rows_ref, out_ref, image_ref):
    @pl.when(pl.program_id(0) == 0)
    def _():
        image_real, image_imag = subgrid_image(
            grid_ref[:, :SG].astype(jnp.bfloat16),
            grid_ref[:, SG:].astype(jnp.bfloat16),
            dft_ref[:, :SG],
            dft_ref[:, SG:],
        )
        image_ref[:SG, :SG] = image_real
        image_ref[:SG, SG:] = -image_imag
        image_ref[SG:, :SG] = image_imag
        image_ref[SG:, SG:] = image_real

    me = lax.axis_index("sub").astype(jnp.float32)

    def one_chunk(index, unused):
        here = pl.ds(pl.multiple_of(index * CHUNK, CHUNK), CHUNK)
        match = rows_ref[0, 0:1, here] == me
        hit = jnp.max(match.astype(jnp.float32)) > 0.0

        @pl.when(hit)
        def _():
            coarse_u, fine_u = powers(rows_ref[0, 1:2, here], CHUNK)
            along_real, along_imag = outer_product(coarse_u, fine_u)
            along = jnp.concatenate(
                [along_real.astype(jnp.bfloat16), along_imag.astype(jnp.bfloat16)]
            )
            inner = plain_dot(image_ref[...], along)
            coarse_v, fine_v = powers(rows_ref[0, 2:3, here], CHUNK)
            ir = inner[:SG].reshape(SG // 8, 8, CHUNK)
            ii = inner[SG:].reshape(SG // 8, 8, CHUNK)
            cr, ci = coarse_v[0][:, None, :], coarse_v[1][:, None, :]
            sum_real = jnp.sum(ir * cr - ii * ci, axis=0)
            sum_imag = jnp.sum(ir * ci + ii * cr, axis=0)
            vis_real = jnp.sum(sum_real * fine_v[0] - sum_imag * fine_v[1], axis=0, keepdims=True)
            vis_imag = jnp.sum(sum_real * fine_v[1] + sum_imag * fine_v[0], axis=0, keepdims=True)
            out_ref[0, :, here] = jnp.where(
                match, jnp.concatenate([vis_real, vis_imag]), 0.0
            )

        @pl.when(jnp.logical_not(hit))
        def _():
            out_ref[0, :, here] = jnp.zeros((2, CHUNK), jnp.float32)

        return unused

    lax.fori_loop(0, rows_ref.shape[2] // CHUNK, one_chunk, 0)


def dft_table():
    spots = np.arange(SG)
    angle = 2.0 * np.pi / SG * (spots[:, None] * spots[None, :] % SG)
    both = np.concatenate([np.cos(angle), np.sin(angle)], axis=1)
    return both.astype(np.float32).astype(jnp.bfloat16)


def local(facet_image, facet_tile, subgrid_cell, row_subgrid, row_uv, observed):
    owners = lax.axis_size("sub")
    rows = row_subgrid.shape[0]
    facet = lax.all_gather(facet_image[0], "sub", axis=0, tiled=True)
    meta = jnp.concatenate([row_subgrid.astype(jnp.float32)[None, :], row_uv], axis=0)
    meta_all = lax.all_gather(meta, "sub", axis=0)
    vmem = pl.BlockSpec(memory_space=pltpu.VMEM)
    smem = pl.BlockSpec(memory_space=pltpu.SMEM)
    terms = pl.pallas_call(
        facet_kernel,
        out_shape=jax.ShapeDtypeStruct((SG, 2 * SG), jnp.float32),
        in_specs=[smem, smem, vmem],
        out_specs=vmem,
        scratch_shapes=[
            pltpu.VMEM((2 * SG, FACET), jnp.bfloat16),
            pltpu.VMEM((2 * SG, FACET), jnp.bfloat16),
        ],
        name="facet_terms",
    )(facet_tile, subgrid_cell, facet)
    grid = lax.psum(terms, "freq")
    partial = pl.pallas_call(
        degrid_kernel,
        grid=(owners,),
        out_shape=jax.ShapeDtypeStruct((owners, 2, rows), jnp.float32),
        in_specs=[
            pl.BlockSpec((SG, 2 * SG), lambda i: (0, 0)),
            pl.BlockSpec((SG, 2 * SG), lambda i: (0, 0)),
            pl.BlockSpec((1, 3, rows), lambda i: (i, 0, 0)),
        ],
        out_specs=pl.BlockSpec((1, 2, rows), lambda i: (i, 0, 0)),
        scratch_shapes=[pltpu.VMEM((2 * SG, 2 * SG), jnp.bfloat16)],
        name="degrid_blocks",
    )(grid, jnp.asarray(dft_table()), meta_all)
    parts = lax.all_to_all(partial, "sub", split_axis=0, concat_axis=0, tiled=True)
    return observed - jnp.sum(parts, axis=0)


def solution(mesh):
    placed = (
        P("freq", "sub", None),
        P("freq", None),
        P("sub", None),
        P(("sub", "freq")),
        P(None, ("sub", "freq")),
        P(None, ("sub", "freq")),
    )
    return jax.shard_map(
        local, mesh=mesh, in_specs=placed, out_specs=P(None, ("sub", "freq")), check_vma=False
    )
```

```python
import functools
import math

import numpy as np
import jax
import jax.numpy as jnp
from jax import lax
from jax.experimental import pallas as pl
from jax.experimental.pallas import tpu as pltpu
from jax.sharding import PartitionSpec as P

SG = 256
FACET = 1024
NIMG = 65536
CHUNK = 256
HALF_PI = math.pi / 2.0


def nt_dot(left, right):
    return lax.dot_general(
        left, right, (((1,), (1,)), ((), ())), preferred_element_type=jnp.float32
    )


def plain_dot(left, right):
    return jnp.dot(left, right, preferred_element_type=jnp.float32)


def unit_root(quarters):
    whole = jnp.floor(quarters + 0.5)
    angle = HALF_PI * (quarters - whole)
    turn = whole.astype(jnp.int32)
    sq = angle * angle
    sin_part = angle * (
        1.0 + sq * (-1.0 / 6.0 + sq * (1.0 / 120.0 + sq * (-1.0 / 5040.0 + sq * (1.0 / 362880.0))))
    )
    cos_part = 1.0 + sq * (
        -0.5 + sq * (1.0 / 24.0 + sq * (-1.0 / 720.0 + sq * (1.0 / 40320.0)))
    )
    odd = (turn & 1) == 1
    cos_turned = jnp.where(odd, sin_part, cos_part)
    sin_turned = jnp.where(odd, cos_part, sin_part)
    cos_out = jnp.where(((turn + 1) & 2) == 2, -cos_turned, cos_turned)
    sin_out = jnp.where((turn & 2) == 2, -sin_turned, sin_turned)
    return cos_out, -sin_out


def outer_product(coarse, fine):
    rows, lanes = coarse[0].shape
    cr, ci = coarse[0][:, None, :], coarse[1][:, None, :]
    fr, fi = fine[0][None, :, :], fine[1][None, :, :]
    real_part = (cr * fr - ci * fi).reshape(rows * 8, lanes)
    imag_part = (cr * fi + ci * fr).reshape(rows * 8, lanes)
    return real_part, imag_part


def window_table(first_cell, first_pixel):
    lanes = lax.broadcasted_iota(jnp.int32, (8, FACET), 1)
    fine_rows = lax.broadcasted_iota(jnp.int32, (8, FACET), 0)
    coarse_lanes = lax.broadcasted_iota(jnp.int32, (SG // 8, FACET), 1)
    coarse_rows = lax.broadcasted_iota(jnp.int32, (SG // 8, FACET), 0)
    position = (2.0 * lanes.astype(jnp.float32) + 1.0) / FACET - 1.0
    weights = 1.0 - 0.75 * position * position
    fine_phase = (fine_rows * (first_pixel + lanes)) & (NIMG - 1)
    coarse_phase = ((first_cell + 8 * coarse_rows) * (first_pixel + coarse_lanes)) & (NIMG - 1)
    fine = unit_root(fine_phase.astype(jnp.float32) * (4.0 / NIMG))
    coarse = unit_root(coarse_phase.astype(jnp.float32) * (4.0 / NIMG))
    real_part, imag_part = outer_product(coarse, (weights * fine[0], weights * fine[1]))
    return real_part.astype(jnp.bfloat16), imag_part.astype(jnp.bfloat16)


def facet_kernel(tile_ref, cell_ref, image_ref, out_ref, col_ref, spectra_ref):
    col_real, col_imag = window_table(cell_ref[0, 0], tile_ref[0, 0] * FACET)
    col_ref[:SG] = col_real
    col_ref[SG:] = col_imag
    for part in range(4):
        rows = slice(part * 256, part * 256 + 256)
        spectra_ref[:, rows] = nt_dot(col_ref[...], image_ref[rows]).astype(jnp.bfloat16)
    row_real, row_imag = window_table(cell_ref[0, 1], tile_ref[0, 1] * FACET)
    first = nt_dot(row_real, spectra_ref[...])
    second = nt_dot(row_imag, spectra_ref[...])
    out_ref[:, :SG] = first[:, :SG] - second[:, SG:]
    out_ref[:, SG:] = first[:, SG:] + second[:, :SG]


def subgrid_image(grid_real, grid_imag, kernel_real, kernel_imag):
    kernel_both = jnp.concatenate([kernel_real, kernel_imag], axis=1)
    first_real = plain_dot(grid_real, kernel_both)
    first_imag = plain_dot(grid_imag, kernel_both)
    half_real = (first_real[:, :SG] - first_imag[:, SG:]).astype(jnp.bfloat16)
    half_imag = (first_real[:, SG:] + first_imag[:, :SG]).astype(jnp.bfloat16)
    half_both = jnp.concatenate([half_real, half_imag], axis=1)
    second_real = plain_dot(kernel_real, half_both)
    second_imag = plain_dot(kernel_imag, half_both)

    def taper(axis):
        cells = lax.broadcasted_iota(jnp.int32, (SG, SG), axis).astype(jnp.float32)
        position = (2.0 * cells + 1.0) / SG - 1.0
        return 1.0 - 0.5 * position * position

    scale = taper(0) * taper(1) / (SG * SG)
    image_real = ((second_real[:, :SG] - second_imag[:, SG:]) * scale).astype(jnp.bfloat16)
    image_imag = ((second_real[:, SG:] + second_imag[:, :SG]) * scale).astype(jnp.bfloat16)
    return image_real, image_imag


def powers(position, lanes):
    quarters = position * (4.0 / SG)
    steps = lax.broadcasted_iota(jnp.int32, (8, lanes), 0).astype(jnp.float32)
    fine = unit_root(quarters * steps)
    mid = unit_root(quarters * (8.0 * steps))
    wide = unit_root(quarters * (64.0 * steps))
    real_parts, imag_parts = [], []
    for q in range(SG // 64):
        wr, wi = wide[0][q : q + 1], wide[1][q : q + 1]
        real_parts.append(mid[0] * wr - mid[1] * wi)
        imag_parts.append(mid[0] * wi + mid[1] * wr)
    return (jnp.concatenate(real_parts), jnp.concatenate(imag_parts)), fine


def degrid_kernel(grid_ref, dft_ref, rows_ref, out_ref, image_ref):
    @pl.when(pl.program_id(0) == 0)
    def _():
        grid_sum = jnp.sum(grid_ref[...], axis=0)
        image_real, image_imag = subgrid_image(
            grid_sum[:, :SG].astype(jnp.bfloat16),
            grid_sum[:, SG:].astype(jnp.bfloat16),
            dft_ref[:, :SG],
            dft_ref[:, SG:],
        )
        image_ref[:SG, :SG] = image_real
        image_ref[:SG, SG:] = -image_imag
        image_ref[SG:, :SG] = image_imag
        image_ref[SG:, SG:] = image_real

    me = lax.axis_index("sub").astype(jnp.float32)

    def one_chunk(index, unused):
        here = pl.ds(pl.multiple_of(index * CHUNK, CHUNK), CHUNK)
        match = rows_ref[0, 0:1, here] == me
        hit = jnp.max(match.astype(jnp.float32)) > 0.0

        @pl.when(hit)
        def _():
            coarse_u, fine_u = powers(rows_ref[0, 1:2, here], CHUNK)
            along_real, along_imag = outer_product(coarse_u, fine_u)
            along = jnp.concatenate(
                [along_real.astype(jnp.bfloat16), along_imag.astype(jnp.bfloat16)]
            )
            inner = plain_dot(image_ref[...], along)
            coarse_v, fine_v = powers(rows_ref[0, 2:3, here], CHUNK)
            ir = inner[:SG].reshape(SG // 8, 8, CHUNK)
            ii = inner[SG:].reshape(SG // 8, 8, CHUNK)
            cr, ci = coarse_v[0][:, None, :], coarse_v[1][:, None, :]
            sum_real = jnp.sum(ir * cr - ii * ci, axis=0)
            sum_imag = jnp.sum(ir * ci + ii * cr, axis=0)
            vis_real = jnp.sum(sum_real * fine_v[0] - sum_imag * fine_v[1], axis=0, keepdims=True)
            vis_imag = jnp.sum(sum_real * fine_v[1] + sum_imag * fine_v[0], axis=0, keepdims=True)
            out_ref[0, :, here] = jnp.where(
                match, jnp.concatenate([vis_real, vis_imag]), 0.0
            )

        @pl.when(jnp.logical_not(hit))
        def _():
            out_ref[0, :, here] = jnp.zeros((2, CHUNK), jnp.float32)

        return unused

    lax.fori_loop(0, rows_ref.shape[2] // CHUNK, one_chunk, 0)


def dft_table():
    spots = np.arange(SG)
    angle = 2.0 * np.pi / SG * (spots[:, None] * spots[None, :] % SG)
    both = np.concatenate([np.cos(angle), np.sin(angle)], axis=1)
    return both.astype(np.float32).astype(jnp.bfloat16)


MESH = pl.DeviceIdType.MESH
PIECES = 3


def gather_kernel(layers, facet_ref, meta_ref, facets_ref, metas_ref, send_sem, recv_sem, own_sem):
    me = lax.axis_index("sub")
    layer = me // 4
    in_layer = me % 4
    pair_y = me - in_layer + (in_layer + 2) % 4
    pair_x = me + 1 - 2 * (me % 2)
    diagonal = me - in_layer + (3 - in_layer)
    above, below = me + 4, me - 4
    has_above = layer < layers - 1
    has_below = layer > 0
    columns = facet_ref.shape[1] // 2

    barrier = pltpu.get_barrier_semaphore()
    for peer in (pair_y, pair_x):
        pl.semaphore_signal(barrier, inc=1, device_id={"sub": peer}, device_id_type=MESH)

    @pl.when(has_above)
    def _():
        pl.semaphore_signal(barrier, inc=1, device_id={"sub": above}, device_id_type=MESH)

    @pl.when(has_below)
    def _():
        pl.semaphore_signal(barrier, inc=1, device_id={"sub": below}, device_id_type=MESH)

    peers = 2 + jnp.minimum(layers - 1 - layer, 1) + jnp.minimum(layer, 1)
    pl.semaphore_wait(barrier, peers)

    def slot(part, index):
        if part == 2:
            return metas_ref.at[index]
        return facets_ref.at[index, :, part * columns : (part + 1) * columns]

    def own(part):
        if part == 2:
            return meta_ref
        return facet_ref.at[:, part * columns : (part + 1) * columns]

    def copy(part, index, kind, peer, first=False):
        return pltpu.make_async_remote_copy(
            src_ref=own(part) if first else slot(part, index),
            dst_ref=slot(part, index),
            send_sem=send_sem.at[kind, part, index],
            recv_sem=recv_sem.at[part, index],
            device_id={"sub": peer},
            device_id_type=MESH,
        )

    def arrived(part, index):
        copy(part, index, 0, pair_y).wait_recv()

    firsts = [(2, pair_y), (3, pair_x)]
    seconds = [(3, pair_x), (2, pair_y), (3, pair_x)]
    partners = [pair_y, pair_x, pair_y]
    others = [pair_x, pair_y, pair_x]

    def distances(run):
        for far in range(1, layers):

            @pl.when(layer >= far)
            def _():
                run(far, -1)

            @pl.when(layer + far < layers)
            def _():
                run(far, 1)

    def onward(act, far, sign):
        index = me + 4 * far * sign

        @pl.when(has_above if sign < 0 else has_below)
        def _():
            for part in range(PIECES):
                act(copy(part, index, 0 if sign < 0 else 1, above if sign < 0 else below))

    start = lambda c: c.start()
    wait_send = lambda c: c.wait_send()

    def line_own(act):
        for part in range(PIECES):
            for kind, peer in firsts:
                act(copy(part, me, kind, peer, True))

        @pl.when(has_above)
        def _():
            for part in range(PIECES):
                act(copy(part, me, 0, above, True))

        @pl.when(has_below)
        def _():
            for part in range(PIECES):
                act(copy(part, me, 1, below, True))

    line_own(start)
    own_facet = pltpu.make_async_copy(facet_ref, facets_ref.at[me], own_sem.at[0])
    own_meta = pltpu.make_async_copy(meta_ref, metas_ref.at[me], own_sem.at[1])
    own_facet.start()
    own_meta.start()

    def second_leg(offset):
        for part in range(PIECES):
            index = partners[part] + offset
            arrived(part, index)
            copy(part, index, seconds[part][0], seconds[part][1]).start()

    def at_distance(far, act):
        @pl.when(layer >= far)
        def _():
            act(far, -1)

        @pl.when(layer + far < layers)
        def _():
            act(far, 1)

    def first_leg(far, sign):
        index = me + 4 * far * sign
        for part in range(PIECES):
            arrived(part, index)
        onward(start, far, sign)
        for part in range(PIECES):
            for kind, peer in firsts:
                copy(part, index, kind, peer).start()

    for far in range(1, layers):
        at_distance(far, first_leg)
        if far == 1:
            second_leg(0)
        else:
            at_distance(far - 1, lambda f, sign: second_leg(4 * f * sign))
    at_distance(layers - 1, lambda f, sign: second_leg(4 * f * sign))

    def last_leg(offset):
        for part in range(PIECES):
            arrived(part, others[part] + offset)
            arrived(part, diagonal + offset)

    last_leg(0)
    distances(lambda far, sign: last_leg(4 * far * sign))

    line_own(wait_send)
    for part in range(PIECES):
        copy(part, partners[part], seconds[part][0], seconds[part][1]).wait_send()

    def drain(far, sign):
        onward(wait_send, far, sign)
        for part in range(PIECES):
            for kind, peer in firsts:
                copy(part, me + 4 * far * sign, kind, peer).wait_send()
            copy(
                part, partners[part] + 4 * far * sign, seconds[part][0], seconds[part][1]
            ).wait_send()

    distances(drain)
    own_facet.wait()
    own_meta.wait()


def scatter_kernel(axis, count, same, parts_ref, out_ref, send_sem, recv_sem, own_sem):
    me = lax.axis_index(axis)
    barrier = pltpu.get_barrier_semaphore()
    for step in range(1, count):
        peer = lax.rem(me + step, count)
        pl.semaphore_signal(barrier, inc=1, device_id={axis: peer}, device_id_type=MESH)
    pl.semaphore_wait(barrier, count - 1)

    def copy(step):
        peer = lax.rem(me + step, count)
        return pltpu.make_async_remote_copy(
            src_ref=parts_ref if same else parts_ref.at[peer],
            dst_ref=out_ref.at[me],
            send_sem=send_sem.at[step],
            recv_sem=recv_sem.at[step],
            device_id={axis: peer},
            device_id_type=MESH,
        )

    for step in range(1, count):
        copy(step).start()
    local_copy = pltpu.make_async_copy(
        parts_ref if same else parts_ref.at[me], out_ref.at[me], own_sem.at[0]
    )
    local_copy.start()
    local_copy.wait()
    for step in range(1, count):
        source = lax.rem(me - step + count, count)
        pltpu.make_async_remote_copy(
            src_ref=parts_ref if same else parts_ref.at[source],
            dst_ref=out_ref.at[source],
            send_sem=send_sem.at[step],
            recv_sem=recv_sem.at[step],
            device_id={axis: source},
            device_id_type=MESH,
        ).wait_recv()
    for step in range(1, count):
        copy(step).wait_send()


def direct_scatter(parts, axis, same, collective_id, name):
    count = lax.axis_size(axis)
    vmem = pl.BlockSpec(memory_space=pltpu.VMEM)
    tail = parts.shape if same else parts.shape[1:]
    return pl.pallas_call(
        functools.partial(scatter_kernel, axis, count, same),
        out_shape=jax.ShapeDtypeStruct((count,) + tail, parts.dtype),
        in_specs=[vmem],
        out_specs=vmem,
        scratch_shapes=[
            pltpu.SemaphoreType.DMA((count,)),
            pltpu.SemaphoreType.DMA((count,)),
            pltpu.SemaphoreType.DMA((1,)),
        ],
        compiler_params=pltpu.CompilerParams(collective_id=collective_id, has_side_effects=True),
        name=name,
    )(parts)


def local(facet_image, facet_tile, subgrid_cell, row_subgrid, row_uv, observed):
    owners = lax.axis_size("sub")
    rows = row_subgrid.shape[0]
    vmem = pl.BlockSpec(memory_space=pltpu.VMEM)
    smem = pl.BlockSpec(memory_space=pltpu.SMEM)
    meta = jnp.concatenate([row_subgrid.astype(jnp.float32)[None, :], row_uv], axis=0)
    facet_shape = facet_image.shape[1:]
    facet, meta_all = pl.pallas_call(
        functools.partial(gather_kernel, owners // 4),
        out_shape=(
            jax.ShapeDtypeStruct((owners,) + facet_shape, facet_image.dtype),
            jax.ShapeDtypeStruct((owners,) + meta.shape, meta.dtype),
        ),
        in_specs=[vmem, vmem],
        out_specs=(vmem, vmem),
        scratch_shapes=[
            pltpu.SemaphoreType.DMA((4, PIECES, owners)),
            pltpu.SemaphoreType.DMA((PIECES, owners)),
            pltpu.SemaphoreType.DMA((2,)),
        ],
        compiler_params=pltpu.CompilerParams(collective_id=0, has_side_effects=True),
        name="gather_rows",
    )(facet_image[0], meta)
    facet = facet.reshape(FACET, FACET)
    terms = pl.pallas_call(
        facet_kernel,
        out_shape=jax.ShapeDtypeStruct((SG, 2 * SG), jnp.float32),
        in_specs=[smem, smem, vmem],
        out_specs=vmem,
        scratch_shapes=[
            pltpu.VMEM((2 * SG, FACET), jnp.bfloat16),
            pltpu.VMEM((2 * SG, FACET), jnp.bfloat16),
        ],
        name="facet_terms",
    )(facet_tile, subgrid_cell, facet)
    both = direct_scatter(terms, "freq", True, 1, "facet_sum")
    partial = pl.pallas_call(
        degrid_kernel,
        grid=(owners,),
        out_shape=jax.ShapeDtypeStruct((owners, 2, rows), jnp.float32),
        in_specs=[
            pl.BlockSpec(both.shape, lambda i: (0, 0, 0)),
            pl.BlockSpec((SG, 2 * SG), lambda i: (0, 0)),
            pl.BlockSpec((1, 3, rows), lambda i: (i, 0, 0)),
        ],
        out_specs=pl.BlockSpec((1, 2, rows), lambda i: (i, 0, 0)),
        scratch_shapes=[pltpu.VMEM((2 * SG, 2 * SG), jnp.bfloat16)],
        name="degrid_blocks",
    )(both, jnp.asarray(dft_table()), meta_all)
    parts = direct_scatter(partial, "sub", False, 2, "return_rows")
    return observed - jnp.sum(parts, axis=0)


def solution(mesh):
    placed = (
        P("freq", "sub", None),
        P("freq", None),
        P("sub", None),
        P(("sub", "freq")),
        P(None, ("sub", "freq")),
        P(None, ("sub", "freq")),
    )
    return jax.shard_map(
        local, mesh=mesh, in_specs=placed, out_specs=P(None, ("sub", "freq")), check_vma=False
    )
```

```python
import functools
import math

import numpy as np
import jax
import jax.numpy as jnp
from jax import lax
from jax.experimental import pallas as pl
from jax.experimental.pallas import tpu as pltpu
from jax.sharding import PartitionSpec as P

SG = 256
FACET = 1024
NIMG = 65536
CHUNK = 256
HALF_PI = math.pi / 2.0


def nt_dot(left, right):
    return lax.dot_general(
        left, right, (((1,), (1,)), ((), ())), preferred_element_type=jnp.float32
    )


def plain_dot(left, right):
    return jnp.dot(left, right, preferred_element_type=jnp.float32)


def unit_root(quarters):
    whole = jnp.floor(quarters + 0.5)
    angle = HALF_PI * (quarters - whole)
    turn = whole.astype(jnp.int32)
    sq = angle * angle
    sin_part = angle * (
        1.0 + sq * (-1.0 / 6.0 + sq * (1.0 / 120.0 + sq * (-1.0 / 5040.0 + sq * (1.0 / 362880.0))))
    )
    cos_part = 1.0 + sq * (
        -0.5 + sq * (1.0 / 24.0 + sq * (-1.0 / 720.0 + sq * (1.0 / 40320.0)))
    )
    odd = (turn & 1) == 1
    cos_turned = jnp.where(odd, sin_part, cos_part)
    sin_turned = jnp.where(odd, cos_part, sin_part)
    cos_out = jnp.where(((turn + 1) & 2) == 2, -cos_turned, cos_turned)
    sin_out = jnp.where((turn & 2) == 2, -sin_turned, sin_turned)
    return cos_out, -sin_out


def outer_product(coarse, fine):
    rows, lanes = coarse[0].shape
    cr, ci = coarse[0][:, None, :], coarse[1][:, None, :]
    fr, fi = fine[0][None, :, :], fine[1][None, :, :]
    real_part = (cr * fr - ci * fi).reshape(rows * 8, lanes)
    imag_part = (cr * fi + ci * fr).reshape(rows * 8, lanes)
    return real_part, imag_part


def window_table(first_cell, first_pixel):
    lanes = lax.broadcasted_iota(jnp.int32, (8, FACET), 1)
    fine_rows = lax.broadcasted_iota(jnp.int32, (8, FACET), 0)
    coarse_lanes = lax.broadcasted_iota(jnp.int32, (SG // 8, FACET), 1)
    coarse_rows = lax.broadcasted_iota(jnp.int32, (SG // 8, FACET), 0)
    position = (2.0 * lanes.astype(jnp.float32) + 1.0) / FACET - 1.0
    weights = 1.0 - 0.75 * position * position
    fine_phase = (fine_rows * (first_pixel + lanes)) & (NIMG - 1)
    coarse_phase = ((first_cell + 8 * coarse_rows) * (first_pixel + coarse_lanes)) & (NIMG - 1)
    fine = unit_root(fine_phase.astype(jnp.float32) * (4.0 / NIMG))
    coarse = unit_root(coarse_phase.astype(jnp.float32) * (4.0 / NIMG))
    real_part, imag_part = outer_product(coarse, (weights * fine[0], weights * fine[1]))
    return real_part.astype(jnp.bfloat16), imag_part.astype(jnp.bfloat16)


def facet_kernel(tile_ref, cell_ref, image_ref, out_ref, col_ref, spectra_ref):
    col_real, col_imag = window_table(cell_ref[0, 0], tile_ref[0, 0] * FACET)
    col_ref[:SG] = col_real
    col_ref[SG:] = col_imag
    for part in range(4):
        rows = slice(part * 256, part * 256 + 256)
        spectra_ref[:, rows] = nt_dot(col_ref[...], image_ref[rows]).astype(jnp.bfloat16)
    row_real, row_imag = window_table(cell_ref[0, 1], tile_ref[0, 1] * FACET)
    first = nt_dot(row_real, spectra_ref[...])
    second = nt_dot(row_imag, spectra_ref[...])
    out_ref[:, :SG] = first[:, :SG] - second[:, SG:]
    out_ref[:, SG:] = first[:, SG:] + second[:, :SG]


def subgrid_image(grid_real, grid_imag, kernel_real, kernel_imag):
    kernel_both = jnp.concatenate([kernel_real, kernel_imag], axis=1)
    first_real = plain_dot(grid_real, kernel_both)
    first_imag = plain_dot(grid_imag, kernel_both)
    half_real = (first_real[:, :SG] - first_imag[:, SG:]).astype(jnp.bfloat16)
    half_imag = (first_real[:, SG:] + first_imag[:, :SG]).astype(jnp.bfloat16)
    half_both = jnp.concatenate([half_real, half_imag], axis=1)
    second_real = plain_dot(kernel_real, half_both)
    second_imag = plain_dot(kernel_imag, half_both)

    def taper(axis):
        cells = lax.broadcasted_iota(jnp.int32, (SG, SG), axis).astype(jnp.float32)
        position = (2.0 * cells + 1.0) / SG - 1.0
        return 1.0 - 0.5 * position * position

    scale = taper(0) * taper(1) / (SG * SG)
    image_real = ((second_real[:, :SG] - second_imag[:, SG:]) * scale).astype(jnp.bfloat16)
    image_imag = ((second_real[:, SG:] + second_imag[:, :SG]) * scale).astype(jnp.bfloat16)
    return image_real, image_imag


def eighth_power(root):
    real_part, imag_part = root
    for _ in range(3):
        real_part, imag_part = (
            real_part * real_part - imag_part * imag_part,
            2.0 * real_part * imag_part,
        )
    return real_part, imag_part


def powers(position, lanes):
    quarters = position * (4.0 / SG)
    steps = lax.broadcasted_iota(jnp.int32, (8, lanes), 0).astype(jnp.float32)
    fine = unit_root(quarters * steps)
    mid = eighth_power(fine)
    wide = eighth_power(mid)
    real_parts, imag_parts = [], []
    for q in range(SG // 64):
        wr, wi = wide[0][q : q + 1], wide[1][q : q + 1]
        real_parts.append(mid[0] * wr - mid[1] * wi)
        imag_parts.append(mid[0] * wi + mid[1] * wr)
    return (jnp.concatenate(real_parts), jnp.concatenate(imag_parts)), fine


def permutation(rank):
    count = rank.shape[1]
    places = lax.broadcasted_iota(jnp.int32, (count, count), 0).astype(jnp.float32)
    return jnp.where(places == rank, 1.0, 0.0).astype(jnp.bfloat16)


def exact_move(values, product):
    high = values.astype(jnp.bfloat16)
    rest = values - high.astype(jnp.float32)
    mid = rest.astype(jnp.bfloat16)
    low = (rest - mid.astype(jnp.float32)).astype(jnp.bfloat16)
    return (product(high) + product(mid)) + product(low)


def sort_kernel(labels_ref, uv_ref, meta_ref, rank_ref):
    labels = labels_ref[...].astype(jnp.float32)
    count = labels.shape[1]
    spots = lax.broadcasted_iota(jnp.int32, (1, count), 1).astype(jnp.float32)
    keys = labels * count + spots
    turned = jnp.transpose(jnp.broadcast_to(keys, (128, count)))[:, 0:1]
    rank = jnp.sum(jnp.where(turned < keys, 1.0, 0.0), axis=0, keepdims=True)
    rank_ref[...] = rank
    chosen = permutation(rank)
    values = jnp.concatenate([labels, uv_ref[...], jnp.zeros((5, count), jnp.float32)])
    meta_ref[...] = exact_move(values, lambda part: nt_dot(part, chosen))[:3]


def finish_kernel(parts_ref, rank_ref, observed_ref, out_ref):
    total = jnp.sum(parts_ref[...], axis=0)
    padded = jnp.concatenate([total, jnp.zeros((6, total.shape[1]), jnp.float32)])
    chosen = permutation(rank_ref[...])
    out_ref[...] = observed_ref[...] - exact_move(padded, lambda part: plain_dot(part, chosen))[:2]


def degrid_kernel(hit_ref, grid_ref, dft_ref, rows_ref, out_ref, image_ref):
    out_ref[...] = jnp.zeros_like(out_ref)
    grid_sum = jnp.sum(grid_ref[...], axis=0)
    image_real, image_imag = subgrid_image(
        grid_sum[:, :SG].astype(jnp.bfloat16),
        grid_sum[:, SG:].astype(jnp.bfloat16),
        dft_ref[:, :SG],
        dft_ref[:, SG:],
    )
    image_ref[:SG, :SG] = image_real
    image_ref[:SG, SG:] = -image_imag
    image_ref[SG:, :SG] = image_imag
    image_ref[SG:, SG:] = image_real

    me = lax.axis_index("sub").astype(jnp.float32)
    per_block = rows_ref.shape[2] // CHUNK

    def one_chunk(index, unused):
        block = index // per_block
        here = pl.ds(pl.multiple_of((index % per_block) * CHUNK, CHUNK), CHUNK)

        @pl.when(hit_ref[index] > 0)
        def _():
            match = rows_ref[block, 0:1, here] == me
            coarse_u, fine_u = powers(rows_ref[block, 1:2, here], CHUNK)
            along_real, along_imag = outer_product(coarse_u, fine_u)
            along = jnp.concatenate(
                [along_real.astype(jnp.bfloat16), along_imag.astype(jnp.bfloat16)]
            )
            inner = plain_dot(image_ref[...], along)
            coarse_v, fine_v = powers(rows_ref[block, 2:3, here], CHUNK)
            ir = inner[:SG].reshape(SG // 8, 8, CHUNK)
            ii = inner[SG:].reshape(SG // 8, 8, CHUNK)
            cr, ci = coarse_v[0][:, None, :], coarse_v[1][:, None, :]
            sum_real = jnp.sum(ir * cr - ii * ci, axis=0)
            sum_imag = jnp.sum(ir * ci + ii * cr, axis=0)
            vis_real = jnp.sum(sum_real * fine_v[0] - sum_imag * fine_v[1], axis=0, keepdims=True)
            vis_imag = jnp.sum(sum_real * fine_v[1] + sum_imag * fine_v[0], axis=0, keepdims=True)
            out_ref[block, :, here] = jnp.where(
                match, jnp.concatenate([vis_real, vis_imag]), 0.0
            )

        return unused

    lax.fori_loop(0, rows_ref.shape[0] * per_block, one_chunk, 0)


def dft_table():
    spots = np.arange(SG)
    angle = 2.0 * np.pi / SG * (spots[:, None] * spots[None, :] % SG)
    both = np.concatenate([np.cos(angle), np.sin(angle)], axis=1)
    return both.astype(np.float32).astype(jnp.bfloat16)


MESH = pl.DeviceIdType.MESH
PIECES = 3


def gather_kernel(layers, facet_ref, meta_ref, facets_ref, metas_ref, send_sem, recv_sem, own_sem):
    me = lax.axis_index("sub")
    layer = me // 4
    in_layer = me % 4
    pair_y = me - in_layer + (in_layer + 2) % 4
    pair_x = me + 1 - 2 * (me % 2)
    diagonal = me - in_layer + (3 - in_layer)
    above, below = me + 4, me - 4
    has_above = layer < layers - 1
    has_below = layer > 0
    columns = facet_ref.shape[1] // 2

    barrier = pltpu.get_barrier_semaphore()
    for peer in (pair_y, pair_x):
        pl.semaphore_signal(barrier, inc=1, device_id={"sub": peer}, device_id_type=MESH)

    @pl.when(has_above)
    def _():
        pl.semaphore_signal(barrier, inc=1, device_id={"sub": above}, device_id_type=MESH)

    @pl.when(has_below)
    def _():
        pl.semaphore_signal(barrier, inc=1, device_id={"sub": below}, device_id_type=MESH)

    peers = 2 + jnp.minimum(layers - 1 - layer, 1) + jnp.minimum(layer, 1)
    pl.semaphore_wait(barrier, peers)

    def slot(part, index):
        if part == 2:
            return metas_ref.at[index]
        return facets_ref.at[index, :, part * columns : (part + 1) * columns]

    def own(part):
        if part == 2:
            return meta_ref
        return facet_ref.at[:, part * columns : (part + 1) * columns]

    def copy(part, index, kind, peer, first=False):
        return pltpu.make_async_remote_copy(
            src_ref=own(part) if first else slot(part, index),
            dst_ref=slot(part, index),
            send_sem=send_sem.at[kind, part, index],
            recv_sem=recv_sem.at[part, index],
            device_id={"sub": peer},
            device_id_type=MESH,
        )

    def arrived(part, index):
        copy(part, index, 0, pair_y).wait_recv()

    firsts = [(2, pair_y), (3, pair_x)]
    seconds = [(3, pair_x), (2, pair_y), (3, pair_x)]
    partners = [pair_y, pair_x, pair_y]
    others = [pair_x, pair_y, pair_x]

    def distances(run):
        for far in range(1, layers):

            @pl.when(layer >= far)
            def _():
                run(far, -1)

            @pl.when(layer + far < layers)
            def _():
                run(far, 1)

    def onward(act, far, sign):
        index = me + 4 * far * sign

        @pl.when(has_above if sign < 0 else has_below)
        def _():
            for part in range(PIECES):
                act(copy(part, index, 0 if sign < 0 else 1, above if sign < 0 else below))

    start = lambda c: c.start()
    wait_send = lambda c: c.wait_send()

    def line_own(act):
        for part in range(PIECES):
            for kind, peer in firsts:
                act(copy(part, me, kind, peer, True))

        @pl.when(has_above)
        def _():
            for part in range(PIECES):
                act(copy(part, me, 0, above, True))

        @pl.when(has_below)
        def _():
            for part in range(PIECES):
                act(copy(part, me, 1, below, True))

    line_own(start)
    own_facet = pltpu.make_async_copy(facet_ref, facets_ref.at[me], own_sem.at[0])
    own_meta = pltpu.make_async_copy(meta_ref, metas_ref.at[me], own_sem.at[1])
    own_facet.start()
    own_meta.start()

    def second_leg(offset):
        for part in range(PIECES):
            index = partners[part] + offset
            arrived(part, index)
            copy(part, index, seconds[part][0], seconds[part][1]).start()

    def at_distance(far, act):
        @pl.when(layer >= far)
        def _():
            act(far, -1)

        @pl.when(layer + far < layers)
        def _():
            act(far, 1)

    def first_leg(far, sign):
        index = me + 4 * far * sign
        for part in range(PIECES):
            arrived(part, index)
        onward(start, far, sign)
        for part in range(PIECES):
            for kind, peer in firsts:
                copy(part, index, kind, peer).start()

    for far in range(1, layers):
        at_distance(far, first_leg)
        if far == 1:
            second_leg(0)
        else:
            at_distance(far - 1, lambda f, sign: second_leg(4 * f * sign))
    at_distance(layers - 1, lambda f, sign: second_leg(4 * f * sign))

    def last_leg(offset):
        for part in range(PIECES):
            arrived(part, others[part] + offset)
            arrived(part, diagonal + offset)

    last_leg(0)
    distances(lambda far, sign: last_leg(4 * far * sign))

    line_own(wait_send)
    for part in range(PIECES):
        copy(part, partners[part], seconds[part][0], seconds[part][1]).wait_send()

    def drain(far, sign):
        onward(wait_send, far, sign)
        for part in range(PIECES):
            for kind, peer in firsts:
                copy(part, me + 4 * far * sign, kind, peer).wait_send()
            copy(
                part, partners[part] + 4 * far * sign, seconds[part][0], seconds[part][1]
            ).wait_send()

    distances(drain)
    own_facet.wait()
    own_meta.wait()


def scatter_kernel(axis, count, same, parts_ref, out_ref, send_sem, recv_sem, own_sem):
    me = lax.axis_index(axis)
    barrier = pltpu.get_barrier_semaphore()
    for step in range(1, count):
        peer = lax.rem(me + step, count)
        pl.semaphore_signal(barrier, inc=1, device_id={axis: peer}, device_id_type=MESH)
    pl.semaphore_wait(barrier, count - 1)

    def copy(step):
        peer = lax.rem(me + step, count)
        return pltpu.make_async_remote_copy(
            src_ref=parts_ref if same else parts_ref.at[peer],
            dst_ref=out_ref.at[me],
            send_sem=send_sem.at[step],
            recv_sem=recv_sem.at[step],
            device_id={axis: peer},
            device_id_type=MESH,
        )

    for step in range(1, count):
        copy(step).start()
    local_copy = pltpu.make_async_copy(
        parts_ref if same else parts_ref.at[me], out_ref.at[me], own_sem.at[0]
    )
    local_copy.start()
    local_copy.wait()
    for step in range(1, count):
        source = lax.rem(me - step + count, count)
        pltpu.make_async_remote_copy(
            src_ref=parts_ref if same else parts_ref.at[source],
            dst_ref=out_ref.at[source],
            send_sem=send_sem.at[step],
            recv_sem=recv_sem.at[step],
            device_id={axis: source},
            device_id_type=MESH,
        ).wait_recv()
    for step in range(1, count):
        copy(step).wait_send()


def direct_scatter(parts, axis, same, collective_id, name):
    count = lax.axis_size(axis)
    vmem = pl.BlockSpec(memory_space=pltpu.VMEM)
    tail = parts.shape if same else parts.shape[1:]
    return pl.pallas_call(
        functools.partial(scatter_kernel, axis, count, same),
        out_shape=jax.ShapeDtypeStruct((count,) + tail, parts.dtype),
        in_specs=[vmem],
        out_specs=vmem,
        scratch_shapes=[
            pltpu.SemaphoreType.DMA((count,)),
            pltpu.SemaphoreType.DMA((count,)),
            pltpu.SemaphoreType.DMA((1,)),
        ],
        compiler_params=pltpu.CompilerParams(collective_id=collective_id, has_side_effects=True),
        name=name,
    )(parts)


def local(facet_image, facet_tile, subgrid_cell, row_subgrid, row_uv, observed):
    owners = lax.axis_size("sub")
    rows = row_subgrid.shape[0]
    vmem = pl.BlockSpec(memory_space=pltpu.VMEM)
    smem = pl.BlockSpec(memory_space=pltpu.SMEM)
    meta, rank = pl.pallas_call(
        sort_kernel,
        out_shape=(
            jax.ShapeDtypeStruct((3, rows), jnp.float32),
            jax.ShapeDtypeStruct((1, rows), jnp.float32),
        ),
        in_specs=[vmem, vmem],
        out_specs=(vmem, vmem),
        name="sort_rows",
    )(row_subgrid[None, :], row_uv)
    facet_shape = facet_image.shape[1:]
    facet, meta_all = pl.pallas_call(
        functools.partial(gather_kernel, owners // 4),
        out_shape=(
            jax.ShapeDtypeStruct((owners,) + facet_shape, facet_image.dtype),
            jax.ShapeDtypeStruct((owners,) + meta.shape, meta.dtype),
        ),
        in_specs=[vmem, vmem],
        out_specs=(vmem, vmem),
        scratch_shapes=[
            pltpu.SemaphoreType.DMA((4, PIECES, owners)),
            pltpu.SemaphoreType.DMA((PIECES, owners)),
            pltpu.SemaphoreType.DMA((2,)),
        ],
        compiler_params=pltpu.CompilerParams(collective_id=0, has_side_effects=True),
        name="gather_rows",
    )(facet_image[0], meta)
    facet = facet.reshape(FACET, FACET)
    terms = pl.pallas_call(
        facet_kernel,
        out_shape=jax.ShapeDtypeStruct((SG, 2 * SG), jnp.float32),
        in_specs=[smem, smem, vmem],
        out_specs=vmem,
        scratch_shapes=[
            pltpu.VMEM((2 * SG, FACET), jnp.bfloat16),
            pltpu.VMEM((2 * SG, FACET), jnp.bfloat16),
        ],
        name="facet_terms",
    )(facet_tile, subgrid_cell, facet)
    both = direct_scatter(terms, "freq", True, 1, "facet_sum")
    here = meta_all[:, 0, :].reshape(-1, CHUNK) == lax.axis_index("sub").astype(jnp.float32)
    hits = jnp.max(here.astype(jnp.int32), axis=1)
    partial = pl.pallas_call(
        degrid_kernel,
        out_shape=jax.ShapeDtypeStruct((owners, 2, rows), jnp.float32),
        in_specs=[smem, vmem, vmem, vmem],
        out_specs=vmem,
        scratch_shapes=[pltpu.VMEM((2 * SG, 2 * SG), jnp.bfloat16)],
        name="degrid_blocks",
    )(hits, both, jnp.asarray(dft_table()), meta_all)
    parts = direct_scatter(partial, "sub", False, 2, "return_rows")
    return pl.pallas_call(
        finish_kernel,
        out_shape=jax.ShapeDtypeStruct((2, rows), jnp.float32),
        in_specs=[vmem, vmem, vmem],
        out_specs=vmem,
        name="residual_rows",
    )(parts, rank, observed)


def solution(mesh):
    placed = (
        P("freq", "sub", None),
        P("freq", None),
        P("sub", None),
        P(("sub", "freq")),
        P(None, ("sub", "freq")),
        P(None, ("sub", "freq")),
    )
    return jax.shard_map(
        local, mesh=mesh, in_specs=placed, out_specs=P(None, ("sub", "freq")), check_vma=False
    )
```

```python
import functools
import math

import numpy as np
import jax
import jax.numpy as jnp
from jax import lax
from jax.experimental import pallas as pl
from jax.experimental.pallas import tpu as pltpu
from jax.sharding import PartitionSpec as P

SG = 256
FACET = 1024
NIMG = 65536
CHUNK = 256
HALF_PI = math.pi / 2.0


def nt_dot(left, right):
    return lax.dot_general(
        left, right, (((1,), (1,)), ((), ())), preferred_element_type=jnp.float32
    )


def plain_dot(left, right):
    return jnp.dot(left, right, preferred_element_type=jnp.float32)


def unit_root(quarters):
    whole = jnp.floor(quarters + 0.5)
    angle = HALF_PI * (quarters - whole)
    turn = whole.astype(jnp.int32)
    sq = angle * angle
    sin_part = angle * (
        1.0 + sq * (-1.0 / 6.0 + sq * (1.0 / 120.0 + sq * (-1.0 / 5040.0 + sq * (1.0 / 362880.0))))
    )
    cos_part = 1.0 + sq * (
        -0.5 + sq * (1.0 / 24.0 + sq * (-1.0 / 720.0 + sq * (1.0 / 40320.0)))
    )
    odd = (turn & 1) == 1
    cos_turned = jnp.where(odd, sin_part, cos_part)
    sin_turned = jnp.where(odd, cos_part, sin_part)
    cos_out = jnp.where(((turn + 1) & 2) == 2, -cos_turned, cos_turned)
    sin_out = jnp.where((turn & 2) == 2, -sin_turned, sin_turned)
    return cos_out, -sin_out


def outer_product(coarse, fine):
    rows, lanes = coarse[0].shape
    cr, ci = coarse[0][:, None, :], coarse[1][:, None, :]
    fr, fi = fine[0][None, :, :], fine[1][None, :, :]
    real_part = (cr * fr - ci * fi).reshape(rows * 8, lanes)
    imag_part = (cr * fi + ci * fr).reshape(rows * 8, lanes)
    return real_part, imag_part


def window_table(first_cell, first_pixel):
    lanes = lax.broadcasted_iota(jnp.int32, (8, FACET), 1)
    fine_rows = lax.broadcasted_iota(jnp.int32, (8, FACET), 0)
    coarse_lanes = lax.broadcasted_iota(jnp.int32, (SG // 8, FACET), 1)
    coarse_rows = lax.broadcasted_iota(jnp.int32, (SG // 8, FACET), 0)
    position = (2.0 * lanes.astype(jnp.float32) + 1.0) / FACET - 1.0
    weights = 1.0 - 0.75 * position * position
    fine_phase = (fine_rows * (first_pixel + lanes)) & (NIMG - 1)
    coarse_phase = ((first_cell + 8 * coarse_rows) * (first_pixel + coarse_lanes)) & (NIMG - 1)
    fine = unit_root(fine_phase.astype(jnp.float32) * (4.0 / NIMG))
    coarse = unit_root(coarse_phase.astype(jnp.float32) * (4.0 / NIMG))
    real_part, imag_part = outer_product(coarse, (weights * fine[0], weights * fine[1]))
    return real_part.astype(jnp.bfloat16), imag_part.astype(jnp.bfloat16)


def facet_kernel(table_ref, image_ref, rows_ref, out_ref, hit_ref, spectra_ref):
    me = lax.axis_index("sub").astype(jnp.float32)
    here = jnp.where(rows_ref[:, 0, :] == me, 1, 0)
    for chunk in range(hit_ref.shape[1]):
        part = here[:, chunk * CHUNK : (chunk + 1) * CHUNK]
        hit_ref[:, chunk : chunk + 1] = jnp.max(part, axis=1, keepdims=True)
    for part in range(4):
        rows = slice(part * 256, part * 256 + 256)
        spectra_ref[:, rows] = nt_dot(table_ref[: 2 * SG], image_ref[rows]).astype(jnp.bfloat16)
    first = nt_dot(table_ref[2 * SG : 3 * SG], spectra_ref[...])
    second = nt_dot(table_ref[3 * SG :], spectra_ref[...])
    out_ref[:, :SG] = first[:, :SG] - second[:, SG:]
    out_ref[:, SG:] = first[:, SG:] + second[:, :SG]


def subgrid_image(grid_real, grid_imag, kernel_real, kernel_imag):
    kernel_both = jnp.concatenate([kernel_real, kernel_imag], axis=1)
    first_real = plain_dot(grid_real, kernel_both)
    first_imag = plain_dot(grid_imag, kernel_both)
    half_real = (first_real[:, :SG] - first_imag[:, SG:]).astype(jnp.bfloat16)
    half_imag = (first_real[:, SG:] + first_imag[:, :SG]).astype(jnp.bfloat16)
    half_both = jnp.concatenate([half_real, half_imag], axis=1)
    second_real = plain_dot(kernel_real, half_both)
    second_imag = plain_dot(kernel_imag, half_both)

    def taper(axis):
        cells = lax.broadcasted_iota(jnp.int32, (SG, SG), axis).astype(jnp.float32)
        position = (2.0 * cells + 1.0) / SG - 1.0
        return 1.0 - 0.5 * position * position

    scale = taper(0) * taper(1) / (SG * SG)
    image_real = ((second_real[:, :SG] - second_imag[:, SG:]) * scale).astype(jnp.bfloat16)
    image_imag = ((second_real[:, SG:] + second_imag[:, :SG]) * scale).astype(jnp.bfloat16)
    return image_real, image_imag


def eighth_power(root):
    real_part, imag_part = root
    for _ in range(3):
        real_part, imag_part = (
            real_part * real_part - imag_part * imag_part,
            2.0 * real_part * imag_part,
        )
    return real_part, imag_part


def powers(position, lanes):
    quarters = position * (4.0 / SG)
    steps = lax.broadcasted_iota(jnp.int32, (8, lanes), 0).astype(jnp.float32)
    fine = unit_root(quarters * steps)
    mid = eighth_power(fine)
    wide = eighth_power(mid)
    real_parts, imag_parts = [], []
    for q in range(SG // 64):
        wr, wi = wide[0][q : q + 1], wide[1][q : q + 1]
        real_parts.append(mid[0] * wr - mid[1] * wi)
        imag_parts.append(mid[0] * wi + mid[1] * wr)
    return (jnp.concatenate(real_parts), jnp.concatenate(imag_parts)), fine


def permutation(rank):
    count = rank.shape[1]
    places = lax.broadcasted_iota(jnp.int32, (count, count), 0).astype(jnp.float32)
    return jnp.where(places == rank, 1.0, 0.0).astype(jnp.bfloat16)


def exact_move(values, product):
    high = values.astype(jnp.bfloat16)
    rest = values - high.astype(jnp.float32)
    mid = rest.astype(jnp.bfloat16)
    low = (rest - mid.astype(jnp.float32)).astype(jnp.bfloat16)
    return (product(high) + product(mid)) + product(low)


def sort_kernel(labels_ref, uv_ref, meta_ref, rank_ref):
    labels = labels_ref[...].astype(jnp.float32)
    count = labels.shape[1]
    spots = lax.broadcasted_iota(jnp.int32, (1, count), 1).astype(jnp.float32)
    keys = labels * count + spots
    turned = jnp.transpose(jnp.broadcast_to(keys, (128, count)))[:, 0:1]
    rank = jnp.sum(jnp.where(turned < keys, 1.0, 0.0), axis=0, keepdims=True)
    rank_ref[...] = rank
    chosen = permutation(rank)
    values = jnp.concatenate([labels, uv_ref[...], jnp.zeros((5, count), jnp.float32)])
    meta_ref[...] = exact_move(values, lambda part: nt_dot(part, chosen))[:3]


def finish_kernel(parts_ref, rank_ref, observed_ref, out_ref):
    total = jnp.sum(parts_ref[...], axis=0)
    padded = jnp.concatenate([total, jnp.zeros((6, total.shape[1]), jnp.float32)])
    chosen = permutation(rank_ref[...])
    out_ref[...] = observed_ref[...] - exact_move(padded, lambda part: plain_dot(part, chosen))[:2]


def degrid_kernel(hit_ref, grid_ref, dft_ref, rows_ref, out_ref, image_ref):
    out_ref[...] = jnp.zeros_like(out_ref)
    grid_sum = jnp.sum(grid_ref[...], axis=0)
    image_real, image_imag = subgrid_image(
        grid_sum[:, :SG].astype(jnp.bfloat16),
        grid_sum[:, SG:].astype(jnp.bfloat16),
        dft_ref[:, :SG],
        dft_ref[:, SG:],
    )
    image_ref[:SG, :SG] = image_real
    image_ref[:SG, SG:] = -image_imag
    image_ref[SG:, :SG] = image_imag
    image_ref[SG:, SG:] = image_real

    me = lax.axis_index("sub").astype(jnp.float32)
    per_block = rows_ref.shape[2] // CHUNK

    def one_chunk(index, unused):
        block = index // per_block
        here = pl.ds(pl.multiple_of((index % per_block) * CHUNK, CHUNK), CHUNK)

        @pl.when(hit_ref[block, index % per_block] > 0)
        def _():
            match = rows_ref[block, 0:1, here] == me
            coarse_u, fine_u = powers(rows_ref[block, 1:2, here], CHUNK)
            along_real, along_imag = outer_product(coarse_u, fine_u)
            along = jnp.concatenate(
                [along_real.astype(jnp.bfloat16), along_imag.astype(jnp.bfloat16)]
            )
            inner = plain_dot(image_ref[...], along)
            coarse_v, fine_v = powers(rows_ref[block, 2:3, here], CHUNK)
            ir = inner[:SG].reshape(SG // 8, 8, CHUNK)
            ii = inner[SG:].reshape(SG // 8, 8, CHUNK)
            cr, ci = coarse_v[0][:, None, :], coarse_v[1][:, None, :]
            sum_real = jnp.sum(ir * cr - ii * ci, axis=0)
            sum_imag = jnp.sum(ir * ci + ii * cr, axis=0)
            vis_real = jnp.sum(sum_real * fine_v[0] - sum_imag * fine_v[1], axis=0, keepdims=True)
            vis_imag = jnp.sum(sum_real * fine_v[1] + sum_imag * fine_v[0], axis=0, keepdims=True)
            out_ref[block, :, here] = jnp.where(
                match, jnp.concatenate([vis_real, vis_imag]), 0.0
            )

        return unused

    lax.fori_loop(0, rows_ref.shape[0] * per_block, one_chunk, 0)


def dft_table():
    spots = np.arange(SG)
    angle = 2.0 * np.pi / SG * (spots[:, None] * spots[None, :] % SG)
    both = np.concatenate([np.cos(angle), np.sin(angle)], axis=1)
    return both.astype(np.float32).astype(jnp.bfloat16)


MESH = pl.DeviceIdType.MESH
PIECES = 3


def gather_kernel(
    layers, tile_ref, cell_ref, facet_ref, meta_ref, facets_ref, metas_ref, table_ref,
    send_sem, recv_sem, own_sem,
):
    me = lax.axis_index("sub")
    layer = me // 4
    in_layer = me % 4
    pair_y = me - in_layer + (in_layer + 2) % 4
    pair_x = me + 1 - 2 * (me % 2)
    diagonal = me - in_layer + (3 - in_layer)
    above, below = me + 4, me - 4
    has_above = layer < layers - 1
    has_below = layer > 0
    columns = facet_ref.shape[1] // 2

    barrier = pltpu.get_barrier_semaphore()
    for peer in (pair_y, pair_x):
        pl.semaphore_signal(barrier, inc=1, device_id={"sub": peer}, device_id_type=MESH)

    @pl.when(has_above)
    def _():
        pl.semaphore_signal(barrier, inc=1, device_id={"sub": above}, device_id_type=MESH)

    @pl.when(has_below)
    def _():
        pl.semaphore_signal(barrier, inc=1, device_id={"sub": below}, device_id_type=MESH)

    peers = 2 + jnp.minimum(layers - 1 - layer, 1) + jnp.minimum(layer, 1)
    pl.semaphore_wait(barrier, peers)

    def slot(part, index):
        if part == 2:
            return metas_ref.at[index]
        return facets_ref.at[index, :, part * columns : (part + 1) * columns]

    def own(part):
        if part == 2:
            return meta_ref
        return facet_ref.at[:, part * columns : (part + 1) * columns]

    def copy(part, index, kind, peer, first=False):
        return pltpu.make_async_remote_copy(
            src_ref=own(part) if first else slot(part, index),
            dst_ref=slot(part, index),
            send_sem=send_sem.at[kind, part, index],
            recv_sem=recv_sem.at[part, index],
            device_id={"sub": peer},
            device_id_type=MESH,
        )

    def arrived(part, index):
        copy(part, index, 0, pair_y).wait_recv()

    firsts = [(2, pair_y), (3, pair_x)]
    seconds = [(3, pair_x), (2, pair_y), (3, pair_x)]
    partners = [pair_y, pair_x, pair_y]
    others = [pair_x, pair_y, pair_x]

    def distances(run):
        for far in range(1, layers):

            @pl.when(layer >= far)
            def _():
                run(far, -1)

            @pl.when(layer + far < layers)
            def _():
                run(far, 1)

    def onward(act, far, sign):
        index = me + 4 * far * sign

        @pl.when(has_above if sign < 0 else has_below)
        def _():
            for part in range(PIECES):
                act(copy(part, index, 0 if sign < 0 else 1, above if sign < 0 else below))

    start = lambda c: c.start()
    wait_send = lambda c: c.wait_send()

    def line_own(act):
        for part in range(PIECES):
            for kind, peer in firsts:
                act(copy(part, me, kind, peer, True))

        @pl.when(has_above)
        def _():
            for part in range(PIECES):
                act(copy(part, me, 0, above, True))

        @pl.when(has_below)
        def _():
            for part in range(PIECES):
                act(copy(part, me, 1, below, True))

    line_own(start)
    own_facet = pltpu.make_async_copy(facet_ref, facets_ref.at[me], own_sem.at[0])
    own_meta = pltpu.make_async_copy(meta_ref, metas_ref.at[me], own_sem.at[1])
    own_facet.start()
    own_meta.start()
    for axis in range(2):
        real_part, imag_part = window_table(cell_ref[0, axis], tile_ref[0, axis] * FACET)
        table_ref[2 * axis * SG : (2 * axis + 1) * SG] = real_part
        table_ref[(2 * axis + 1) * SG : (2 * axis + 2) * SG] = imag_part

    def second_leg(offset):
        for part in range(PIECES):
            index = partners[part] + offset
            arrived(part, index)
            copy(part, index, seconds[part][0], seconds[part][1]).start()

    def at_distance(far, act):
        @pl.when(layer >= far)
        def _():
            act(far, -1)

        @pl.when(layer + far < layers)
        def _():
            act(far, 1)

    def first_leg(far, sign):
        index = me + 4 * far * sign
        for part in range(PIECES):
            arrived(part, index)
        onward(start, far, sign)
        for part in range(PIECES):
            for kind, peer in firsts:
                copy(part, index, kind, peer).start()

    for far in range(1, layers):
        at_distance(far, first_leg)
        if far == 1:
            second_leg(0)
        else:
            at_distance(far - 1, lambda f, sign: second_leg(4 * f * sign))
    at_distance(layers - 1, lambda f, sign: second_leg(4 * f * sign))

    def last_leg(offset):
        for part in range(PIECES):
            arrived(part, others[part] + offset)
            arrived(part, diagonal + offset)

    last_leg(0)
    distances(lambda far, sign: last_leg(4 * far * sign))

    line_own(wait_send)
    for part in range(PIECES):
        copy(part, partners[part], seconds[part][0], seconds[part][1]).wait_send()

    def drain(far, sign):
        onward(wait_send, far, sign)
        for part in range(PIECES):
            for kind, peer in firsts:
                copy(part, me + 4 * far * sign, kind, peer).wait_send()
            copy(
                part, partners[part] + 4 * far * sign, seconds[part][0], seconds[part][1]
            ).wait_send()

    distances(drain)
    own_facet.wait()
    own_meta.wait()


def scatter_kernel(axis, count, same, parts_ref, out_ref, send_sem, recv_sem, own_sem):
    me = lax.axis_index(axis)
    barrier = pltpu.get_barrier_semaphore()
    for step in range(1, count):
        peer = lax.rem(me + step, count)
        pl.semaphore_signal(barrier, inc=1, device_id={axis: peer}, device_id_type=MESH)
    pl.semaphore_wait(barrier, count - 1)

    def copy(step):
        peer = lax.rem(me + step, count)
        return pltpu.make_async_remote_copy(
            src_ref=parts_ref if same else parts_ref.at[peer],
            dst_ref=out_ref.at[me],
            send_sem=send_sem.at[step],
            recv_sem=recv_sem.at[step],
            device_id={axis: peer},
            device_id_type=MESH,
        )

    for step in range(1, count):
        copy(step).start()
    local_copy = pltpu.make_async_copy(
        parts_ref if same else parts_ref.at[me], out_ref.at[me], own_sem.at[0]
    )
    local_copy.start()
    local_copy.wait()
    for step in range(1, count):
        source = lax.rem(me - step + count, count)
        pltpu.make_async_remote_copy(
            src_ref=parts_ref if same else parts_ref.at[source],
            dst_ref=out_ref.at[source],
            send_sem=send_sem.at[step],
            recv_sem=recv_sem.at[step],
            device_id={axis: source},
            device_id_type=MESH,
        ).wait_recv()
    for step in range(1, count):
        copy(step).wait_send()


def direct_scatter(parts, axis, same, collective_id, name):
    count = lax.axis_size(axis)
    vmem = pl.BlockSpec(memory_space=pltpu.VMEM)
    tail = parts.shape if same else parts.shape[1:]
    return pl.pallas_call(
        functools.partial(scatter_kernel, axis, count, same),
        out_shape=jax.ShapeDtypeStruct((count,) + tail, parts.dtype),
        in_specs=[vmem],
        out_specs=vmem,
        scratch_shapes=[
            pltpu.SemaphoreType.DMA((count,)),
            pltpu.SemaphoreType.DMA((count,)),
            pltpu.SemaphoreType.DMA((1,)),
        ],
        compiler_params=pltpu.CompilerParams(collective_id=collective_id, has_side_effects=True),
        name=name,
    )(parts)


def local(facet_image, facet_tile, subgrid_cell, row_subgrid, row_uv, observed):
    owners = lax.axis_size("sub")
    rows = row_subgrid.shape[0]
    vmem = pl.BlockSpec(memory_space=pltpu.VMEM)
    smem = pl.BlockSpec(memory_space=pltpu.SMEM)
    meta, rank = pl.pallas_call(
        sort_kernel,
        out_shape=(
            jax.ShapeDtypeStruct((3, rows), jnp.float32),
            jax.ShapeDtypeStruct((1, rows), jnp.float32),
        ),
        in_specs=[vmem, vmem],
        out_specs=(vmem, vmem),
        name="sort_rows",
    )(row_subgrid[None, :], row_uv)
    facet_shape = facet_image.shape[1:]
    facet, meta_all, tables = pl.pallas_call(
        functools.partial(gather_kernel, owners // 4),
        out_shape=(
            jax.ShapeDtypeStruct((owners,) + facet_shape, facet_image.dtype),
            jax.ShapeDtypeStruct((owners,) + meta.shape, meta.dtype),
            jax.ShapeDtypeStruct((4 * SG, FACET), jnp.bfloat16),
        ),
        in_specs=[smem, smem, vmem, vmem],
        out_specs=(vmem, vmem, vmem),
        scratch_shapes=[
            pltpu.SemaphoreType.DMA((4, PIECES, owners)),
            pltpu.SemaphoreType.DMA((PIECES, owners)),
            pltpu.SemaphoreType.DMA((2,)),
        ],
        compiler_params=pltpu.CompilerParams(collective_id=0, has_side_effects=True),
        name="gather_rows",
    )(facet_tile, subgrid_cell, facet_image[0], meta)
    facet = facet.reshape(FACET, FACET)
    terms, hits = pl.pallas_call(
        facet_kernel,
        out_shape=(
            jax.ShapeDtypeStruct((SG, 2 * SG), jnp.float32),
            jax.ShapeDtypeStruct((owners, rows // CHUNK), jnp.int32),
        ),
        in_specs=[vmem, vmem, vmem],
        out_specs=(vmem, vmem),
        scratch_shapes=[
            pltpu.VMEM((2 * SG, FACET), jnp.bfloat16),
        ],
        name="facet_terms",
    )(tables, facet, meta_all)
    both = direct_scatter(terms, "freq", True, 1, "facet_sum")
    partial = pl.pallas_call(
        degrid_kernel,
        out_shape=jax.ShapeDtypeStruct((owners, 2, rows), jnp.float32),
        in_specs=[smem, vmem, vmem, vmem],
        out_specs=vmem,
        scratch_shapes=[pltpu.VMEM((2 * SG, 2 * SG), jnp.bfloat16)],
        name="degrid_blocks",
    )(hits, both, jnp.asarray(dft_table()), meta_all)
    parts = direct_scatter(partial, "sub", False, 2, "return_rows")
    return pl.pallas_call(
        finish_kernel,
        out_shape=jax.ShapeDtypeStruct((2, rows), jnp.float32),
        in_specs=[vmem, vmem, vmem],
        out_specs=vmem,
        name="residual_rows",
    )(parts, rank, observed)


def solution(mesh):
    placed = (
        P("freq", "sub", None),
        P("freq", None),
        P("sub", None),
        P(("sub", "freq")),
        P(None, ("sub", "freq")),
        P(None, ("sub", "freq")),
    )
    return jax.shard_map(
        local, mesh=mesh, in_specs=placed, out_specs=P(None, ("sub", "freq")), check_vma=False
    )
```

```python
import functools
import math

import numpy as np
import jax
import jax.numpy as jnp
from jax import lax
from jax.experimental import pallas as pl
from jax.experimental.pallas import tpu as pltpu
from jax.sharding import PartitionSpec as P

SG = 256
FACET = 1024
NIMG = 65536
CHUNK = 128
HALF_PI = math.pi / 2.0


def nt_dot(left, right):
    return lax.dot_general(
        left, right, (((1,), (1,)), ((), ())), preferred_element_type=jnp.float32
    )


def plain_dot(left, right):
    return jnp.dot(left, right, preferred_element_type=jnp.float32)


def unit_root(quarters):
    whole = jnp.floor(quarters + 0.5)
    angle = HALF_PI * (quarters - whole)
    turn = whole.astype(jnp.int32)
    sq = angle * angle
    sin_part = angle * (
        1.0 + sq * (-1.0 / 6.0 + sq * (1.0 / 120.0 + sq * (-1.0 / 5040.0 + sq * (1.0 / 362880.0))))
    )
    cos_part = 1.0 + sq * (
        -0.5 + sq * (1.0 / 24.0 + sq * (-1.0 / 720.0 + sq * (1.0 / 40320.0)))
    )
    odd = (turn & 1) == 1
    cos_turned = jnp.where(odd, sin_part, cos_part)
    sin_turned = jnp.where(odd, cos_part, sin_part)
    cos_out = jnp.where(((turn + 1) & 2) == 2, -cos_turned, cos_turned)
    sin_out = jnp.where((turn & 2) == 2, -sin_turned, sin_turned)
    return cos_out, -sin_out


def outer_product(coarse, fine):
    rows, lanes = coarse[0].shape
    cr, ci = coarse[0][:, None, :], coarse[1][:, None, :]
    fr, fi = fine[0][None, :, :], fine[1][None, :, :]
    real_part = (cr * fr - ci * fi).reshape(rows * 8, lanes)
    imag_part = (cr * fi + ci * fr).reshape(rows * 8, lanes)
    return real_part, imag_part


def window_table(first_cell, first_pixel):
    lanes = lax.broadcasted_iota(jnp.int32, (8, FACET), 1)
    fine_rows = lax.broadcasted_iota(jnp.int32, (8, FACET), 0)
    coarse_lanes = lax.broadcasted_iota(jnp.int32, (SG // 8, FACET), 1)
    coarse_rows = lax.broadcasted_iota(jnp.int32, (SG // 8, FACET), 0)
    position = (2.0 * lanes.astype(jnp.float32) + 1.0) / FACET - 1.0
    weights = 1.0 - 0.75 * position * position
    fine_phase = (fine_rows * (first_pixel + lanes)) & (NIMG - 1)
    coarse_phase = ((first_cell + 8 * coarse_rows) * (first_pixel + coarse_lanes)) & (NIMG - 1)
    fine = unit_root(fine_phase.astype(jnp.float32) * (4.0 / NIMG))
    coarse = unit_root(coarse_phase.astype(jnp.float32) * (4.0 / NIMG))
    real_part, imag_part = outer_product(coarse, (weights * fine[0], weights * fine[1]))
    return real_part.astype(jnp.bfloat16), imag_part.astype(jnp.bfloat16)


def facet_kernel(table_ref, image_ref, rows_ref, out_ref, hit_ref, spectra_ref):
    me = lax.axis_index("sub").astype(jnp.float32)
    here = jnp.where(rows_ref[:, 0, :] == me, 1, 0)
    for chunk in range(hit_ref.shape[1]):
        part = here[:, chunk * CHUNK : (chunk + 1) * CHUNK]
        hit_ref[:, chunk : chunk + 1] = jnp.max(part, axis=1, keepdims=True)
    for part in range(4):
        rows = slice(part * 256, part * 256 + 256)
        spectra_ref[:, rows] = nt_dot(table_ref[: 2 * SG], image_ref[rows]).astype(jnp.bfloat16)
    first = nt_dot(table_ref[2 * SG : 3 * SG], spectra_ref[...])
    second = nt_dot(table_ref[3 * SG :], spectra_ref[...])
    out_ref[:, :SG] = first[:, :SG] - second[:, SG:]
    out_ref[:, SG:] = first[:, SG:] + second[:, :SG]


def subgrid_image(grid_real, grid_imag, kernel_real, kernel_imag):
    kernel_both = jnp.concatenate([kernel_real, kernel_imag], axis=1)
    first_real = plain_dot(grid_real, kernel_both)
    first_imag = plain_dot(grid_imag, kernel_both)
    half_real = (first_real[:, :SG] - first_imag[:, SG:]).astype(jnp.bfloat16)
    half_imag = (first_real[:, SG:] + first_imag[:, :SG]).astype(jnp.bfloat16)
    half_both = jnp.concatenate([half_real, half_imag], axis=1)
    second_real = plain_dot(kernel_real, half_both)
    second_imag = plain_dot(kernel_imag, half_both)

    def taper(axis):
        cells = lax.broadcasted_iota(jnp.int32, (SG, SG), axis).astype(jnp.float32)
        position = (2.0 * cells + 1.0) / SG - 1.0
        return 1.0 - 0.5 * position * position

    scale = taper(0) * taper(1) / (SG * SG)
    image_real = ((second_real[:, :SG] - second_imag[:, SG:]) * scale).astype(jnp.bfloat16)
    image_imag = ((second_real[:, SG:] + second_imag[:, :SG]) * scale).astype(jnp.bfloat16)
    return image_real, image_imag


def eighth_power(root):
    real_part, imag_part = root
    for _ in range(3):
        real_part, imag_part = (
            real_part * real_part - imag_part * imag_part,
            2.0 * real_part * imag_part,
        )
    return real_part, imag_part


def powers(position, lanes):
    quarters = position * (4.0 / SG)
    steps = lax.broadcasted_iota(jnp.int32, (8, lanes), 0).astype(jnp.float32)
    fine = unit_root(quarters * steps)
    mid = eighth_power(fine)
    wide = eighth_power(mid)
    real_parts, imag_parts = [], []
    for q in range(SG // 64):
        wr, wi = wide[0][q : q + 1], wide[1][q : q + 1]
        real_parts.append(mid[0] * wr - mid[1] * wi)
        imag_parts.append(mid[0] * wi + mid[1] * wr)
    return (jnp.concatenate(real_parts), jnp.concatenate(imag_parts)), fine


def permutation(rank):
    count = rank.shape[1]
    places = lax.broadcasted_iota(jnp.int32, (count, count), 0).astype(jnp.float32)
    return jnp.where(places == rank, 1.0, 0.0).astype(jnp.bfloat16)


def exact_move(values, product):
    high = values.astype(jnp.bfloat16)
    rest = values - high.astype(jnp.float32)
    mid = rest.astype(jnp.bfloat16)
    low = (rest - mid.astype(jnp.float32)).astype(jnp.bfloat16)
    return (product(high) + product(mid)) + product(low)


def sort_kernel(labels_ref, uv_ref, meta_ref, rank_ref):
    labels = labels_ref[...].astype(jnp.float32)
    count = labels.shape[1]
    spots = lax.broadcasted_iota(jnp.int32, (1, count), 1).astype(jnp.float32)
    keys = labels * count + spots
    turned = jnp.transpose(jnp.broadcast_to(keys, (128, count)))[:, 0:1]
    rank = jnp.sum(jnp.where(turned < keys, 1.0, 0.0), axis=0, keepdims=True)
    rank_ref[...] = rank
    chosen = permutation(rank)
    values = jnp.concatenate([labels, uv_ref[...], jnp.zeros((5, count), jnp.float32)])
    meta_ref[...] = exact_move(values, lambda part: nt_dot(part, chosen))[:3]


def finish_kernel(parts_ref, rank_ref, observed_ref, out_ref):
    total = jnp.sum(parts_ref[...], axis=0)
    padded = jnp.concatenate([total, jnp.zeros((6, total.shape[1]), jnp.float32)])
    chosen = permutation(rank_ref[...])
    out_ref[...] = observed_ref[...] - exact_move(padded, lambda part: plain_dot(part, chosen))[:2]


def degrid_kernel(hit_ref, grid_ref, dft_ref, rows_ref, out_ref, image_ref):
    out_ref[...] = jnp.zeros_like(out_ref)
    grid_sum = jnp.sum(grid_ref[...], axis=0)
    image_real, image_imag = subgrid_image(
        grid_sum[:, :SG].astype(jnp.bfloat16),
        grid_sum[:, SG:].astype(jnp.bfloat16),
        dft_ref[:, :SG],
        dft_ref[:, SG:],
    )
    image_ref[:SG, :SG] = image_real
    image_ref[:SG, SG:] = -image_imag
    image_ref[SG:, :SG] = image_imag
    image_ref[SG:, SG:] = image_real

    me = lax.axis_index("sub").astype(jnp.float32)
    per_block = rows_ref.shape[2] // CHUNK

    def one_chunk(index, unused):
        block = index // per_block
        here = pl.ds(pl.multiple_of((index % per_block) * CHUNK, CHUNK), CHUNK)

        @pl.when(hit_ref[block, index % per_block] > 0)
        def _():
            match = rows_ref[block, 0:1, here] == me
            coarse_u, fine_u = powers(rows_ref[block, 1:2, here], CHUNK)
            along_real, along_imag = outer_product(coarse_u, fine_u)
            along = jnp.concatenate(
                [along_real.astype(jnp.bfloat16), along_imag.astype(jnp.bfloat16)]
            )
            inner = plain_dot(image_ref[...], along)
            coarse_v, fine_v = powers(rows_ref[block, 2:3, here], CHUNK)
            ir = inner[:SG].reshape(SG // 8, 8, CHUNK)
            ii = inner[SG:].reshape(SG // 8, 8, CHUNK)
            cr, ci = coarse_v[0][:, None, :], coarse_v[1][:, None, :]
            sum_real = jnp.sum(ir * cr - ii * ci, axis=0)
            sum_imag = jnp.sum(ir * ci + ii * cr, axis=0)
            vis_real = jnp.sum(sum_real * fine_v[0] - sum_imag * fine_v[1], axis=0, keepdims=True)
            vis_imag = jnp.sum(sum_real * fine_v[1] + sum_imag * fine_v[0], axis=0, keepdims=True)
            out_ref[block, :, here] = jnp.where(
                match, jnp.concatenate([vis_real, vis_imag]), 0.0
            )

        return unused

    lax.fori_loop(0, rows_ref.shape[0] * per_block, one_chunk, 0)


def dft_table():
    spots = np.arange(SG)
    angle = 2.0 * np.pi / SG * (spots[:, None] * spots[None, :] % SG)
    both = np.concatenate([np.cos(angle), np.sin(angle)], axis=1)
    return both.astype(np.float32).astype(jnp.bfloat16)


MESH = pl.DeviceIdType.MESH
PIECES = 3


def gather_kernel(
    layers, tile_ref, cell_ref, facet_ref, meta_ref, facets_ref, metas_ref, table_ref,
    send_sem, recv_sem, own_sem,
):
    me = lax.axis_index("sub")
    layer = me // 4
    in_layer = me % 4
    pair_y = me - in_layer + (in_layer + 2) % 4
    pair_x = me + 1 - 2 * (me % 2)
    diagonal = me - in_layer + (3 - in_layer)
    above, below = me + 4, me - 4
    has_above = layer < layers - 1
    has_below = layer > 0
    columns = facet_ref.shape[1] // 2

    barrier = pltpu.get_barrier_semaphore()
    for peer in (pair_y, pair_x):
        pl.semaphore_signal(barrier, inc=1, device_id={"sub": peer}, device_id_type=MESH)

    @pl.when(has_above)
    def _():
        pl.semaphore_signal(barrier, inc=1, device_id={"sub": above}, device_id_type=MESH)

    @pl.when(has_below)
    def _():
        pl.semaphore_signal(barrier, inc=1, device_id={"sub": below}, device_id_type=MESH)

    peers = 2 + jnp.minimum(layers - 1 - layer, 1) + jnp.minimum(layer, 1)
    pl.semaphore_wait(barrier, peers)

    def slot(part, index):
        if part == 2:
            return metas_ref.at[index]
        return facets_ref.at[index, :, part * columns : (part + 1) * columns]

    def own(part):
        if part == 2:
            return meta_ref
        return facet_ref.at[:, part * columns : (part + 1) * columns]

    def copy(part, index, kind, peer, first=False):
        return pltpu.make_async_remote_copy(
            src_ref=own(part) if first else slot(part, index),
            dst_ref=slot(part, index),
            send_sem=send_sem.at[kind, part, index],
            recv_sem=recv_sem.at[part, index],
            device_id={"sub": peer},
            device_id_type=MESH,
        )

    def arrived(part, index):
        copy(part, index, 0, pair_y).wait_recv()

    firsts = [(2, pair_y), (3, pair_x)]
    seconds = [(3, pair_x), (2, pair_y), (3, pair_x)]
    partners = [pair_y, pair_x, pair_y]
    others = [pair_x, pair_y, pair_x]

    def distances(run):
        for far in range(1, layers):

            @pl.when(layer >= far)
            def _():
                run(far, -1)

            @pl.when(layer + far < layers)
            def _():
                run(far, 1)

    def onward(act, far, sign):
        index = me + 4 * far * sign

        @pl.when(has_above if sign < 0 else has_below)
        def _():
            for part in range(PIECES):
                act(copy(part, index, 0 if sign < 0 else 1, above if sign < 0 else below))

    start = lambda c: c.start()
    wait_send = lambda c: c.wait_send()

    def line_own(act):
        for part in range(PIECES):
            for kind, peer in firsts:
                act(copy(part, me, kind, peer, True))

        @pl.when(has_above)
        def _():
            for part in range(PIECES):
                act(copy(part, me, 0, above, True))

        @pl.when(has_below)
        def _():
            for part in range(PIECES):
                act(copy(part, me, 1, below, True))

    line_own(start)
    own_facet = pltpu.make_async_copy(facet_ref, facets_ref.at[me], own_sem.at[0])
    own_meta = pltpu.make_async_copy(meta_ref, metas_ref.at[me], own_sem.at[1])
    own_facet.start()
    own_meta.start()
    for axis in range(2):
        real_part, imag_part = window_table(cell_ref[0, axis], tile_ref[0, axis] * FACET)
        table_ref[2 * axis * SG : (2 * axis + 1) * SG] = real_part
        table_ref[(2 * axis + 1) * SG : (2 * axis + 2) * SG] = imag_part

    def second_leg(offset):
        for part in range(PIECES):
            index = partners[part] + offset
            arrived(part, index)
            copy(part, index, seconds[part][0], seconds[part][1]).start()

    def at_distance(far, act):
        @pl.when(layer >= far)
        def _():
            act(far, -1)

        @pl.when(layer + far < layers)
        def _():
            act(far, 1)

    def first_leg(far, sign):
        index = me + 4 * far * sign
        for part in range(PIECES):
            arrived(part, index)
        onward(start, far, sign)
        for part in range(PIECES):
            for kind, peer in firsts:
                copy(part, index, kind, peer).start()

    for far in range(1, layers):
        at_distance(far, first_leg)
        if far == 1:
            second_leg(0)
        else:
            at_distance(far - 1, lambda f, sign: second_leg(4 * f * sign))
    at_distance(layers - 1, lambda f, sign: second_leg(4 * f * sign))

    def last_leg(offset):
        for part in range(PIECES):
            arrived(part, others[part] + offset)
            arrived(part, diagonal + offset)

    last_leg(0)
    distances(lambda far, sign: last_leg(4 * far * sign))

    line_own(wait_send)
    for part in range(PIECES):
        copy(part, partners[part], seconds[part][0], seconds[part][1]).wait_send()

    def drain(far, sign):
        onward(wait_send, far, sign)
        for part in range(PIECES):
            for kind, peer in firsts:
                copy(part, me + 4 * far * sign, kind, peer).wait_send()
            copy(
                part, partners[part] + 4 * far * sign, seconds[part][0], seconds[part][1]
            ).wait_send()

    distances(drain)
    own_facet.wait()
    own_meta.wait()


def scatter_kernel(axis, count, same, parts_ref, out_ref, send_sem, recv_sem, own_sem):
    me = lax.axis_index(axis)
    barrier = pltpu.get_barrier_semaphore()
    for step in range(1, count):
        peer = lax.rem(me + step, count)
        pl.semaphore_signal(barrier, inc=1, device_id={axis: peer}, device_id_type=MESH)
    pl.semaphore_wait(barrier, count - 1)

    def copy(step):
        peer = lax.rem(me + step, count)
        return pltpu.make_async_remote_copy(
            src_ref=parts_ref if same else parts_ref.at[peer],
            dst_ref=out_ref.at[me],
            send_sem=send_sem.at[step],
            recv_sem=recv_sem.at[step],
            device_id={axis: peer},
            device_id_type=MESH,
        )

    for step in range(1, count):
        copy(step).start()
    local_copy = pltpu.make_async_copy(
        parts_ref if same else parts_ref.at[me], out_ref.at[me], own_sem.at[0]
    )
    local_copy.start()
    local_copy.wait()
    for step in range(1, count):
        source = lax.rem(me - step + count, count)
        pltpu.make_async_remote_copy(
            src_ref=parts_ref if same else parts_ref.at[source],
            dst_ref=out_ref.at[source],
            send_sem=send_sem.at[step],
            recv_sem=recv_sem.at[step],
            device_id={axis: source},
            device_id_type=MESH,
        ).wait_recv()
    for step in range(1, count):
        copy(step).wait_send()


def direct_scatter(parts, axis, same, collective_id, name):
    count = lax.axis_size(axis)
    vmem = pl.BlockSpec(memory_space=pltpu.VMEM)
    tail = parts.shape if same else parts.shape[1:]
    return pl.pallas_call(
        functools.partial(scatter_kernel, axis, count, same),
        out_shape=jax.ShapeDtypeStruct((count,) + tail, parts.dtype),
        in_specs=[vmem],
        out_specs=vmem,
        scratch_shapes=[
            pltpu.SemaphoreType.DMA((count,)),
            pltpu.SemaphoreType.DMA((count,)),
            pltpu.SemaphoreType.DMA((1,)),
        ],
        compiler_params=pltpu.CompilerParams(collective_id=collective_id, has_side_effects=True),
        name=name,
    )(parts)


def local(facet_image, facet_tile, subgrid_cell, row_subgrid, row_uv, observed):
    owners = lax.axis_size("sub")
    rows = row_subgrid.shape[0]
    vmem = pl.BlockSpec(memory_space=pltpu.VMEM)
    smem = pl.BlockSpec(memory_space=pltpu.SMEM)
    meta, rank = pl.pallas_call(
        sort_kernel,
        out_shape=(
            jax.ShapeDtypeStruct((3, rows), jnp.float32),
            jax.ShapeDtypeStruct((1, rows), jnp.float32),
        ),
        in_specs=[vmem, vmem],
        out_specs=(vmem, vmem),
        name="sort_rows",
    )(row_subgrid[None, :], row_uv)
    facet_shape = facet_image.shape[1:]
    facet, meta_all, tables = pl.pallas_call(
        functools.partial(gather_kernel, owners // 4),
        out_shape=(
            jax.ShapeDtypeStruct((owners,) + facet_shape, facet_image.dtype),
            jax.ShapeDtypeStruct((owners,) + meta.shape, meta.dtype),
            jax.ShapeDtypeStruct((4 * SG, FACET), jnp.bfloat16),
        ),
        in_specs=[smem, smem, vmem, vmem],
        out_specs=(vmem, vmem, vmem),
        scratch_shapes=[
            pltpu.SemaphoreType.DMA((4, PIECES, owners)),
            pltpu.SemaphoreType.DMA((PIECES, owners)),
            pltpu.SemaphoreType.DMA((2,)),
        ],
        compiler_params=pltpu.CompilerParams(collective_id=0, has_side_effects=True),
        name="gather_rows",
    )(facet_tile, subgrid_cell, facet_image[0], meta)
    facet = facet.reshape(FACET, FACET)
    terms, hits = pl.pallas_call(
        facet_kernel,
        out_shape=(
            jax.ShapeDtypeStruct((SG, 2 * SG), jnp.float32),
            jax.ShapeDtypeStruct((owners, rows // CHUNK), jnp.int32),
        ),
        in_specs=[vmem, vmem, vmem],
        out_specs=(vmem, vmem),
        scratch_shapes=[
            pltpu.VMEM((2 * SG, FACET), jnp.bfloat16),
        ],
        name="facet_terms",
    )(tables, facet, meta_all)
    both = direct_scatter(terms, "freq", True, 1, "facet_sum")
    partial = pl.pallas_call(
        degrid_kernel,
        out_shape=jax.ShapeDtypeStruct((owners, 2, rows), jnp.float32),
        in_specs=[smem, vmem, vmem, vmem],
        out_specs=vmem,
        scratch_shapes=[pltpu.VMEM((2 * SG, 2 * SG), jnp.bfloat16)],
        name="degrid_blocks",
    )(hits, both, jnp.asarray(dft_table()), meta_all)
    parts = direct_scatter(partial, "sub", False, 2, "return_rows")
    return pl.pallas_call(
        finish_kernel,
        out_shape=jax.ShapeDtypeStruct((2, rows), jnp.float32),
        in_specs=[vmem, vmem, vmem],
        out_specs=vmem,
        name="residual_rows",
    )(parts, rank, observed)


def solution(mesh):
    placed = (
        P("freq", "sub", None),
        P("freq", None),
        P("sub", None),
        P(("sub", "freq")),
        P(None, ("sub", "freq")),
        P(None, ("sub", "freq")),
    )
    return jax.shard_map(
        local, mesh=mesh, in_specs=placed, out_specs=P(None, ("sub", "freq")), check_vma=False
    )
```
